256 devices in a mesh: sens: 8 (over x_lo, y), pts: 32 (over z, x_hi, core).
Axes of the slice: x: 4 (x_hi: 2, x_lo: 2; x = x_hi * 2 + x_lo), y: 4, z: 8, core: 2. Of those that a mesh axis runs over, the one named last changes fastest.
Arguments:
- vectors: float32 [4, 1024, 420], P(None, 'pts'), may hold values from -6 to 6
- kernel_hat: float32 [2, 448, 512, 1024], P(None, 'pts', 'sens'), may hold values from -0.1875 to 0.1875
- noise_prec: float32 [512], P(('sens', 'pts')), may hold values from 0.3 to 3
- stencil_coefficients_raw: float32 [1024, 6], P('pts'), may hold values from 0.1 to 2
- offsets: int32 [1024, 6], P('pts'), may hold values from -32 to 32
- amplitude: float32 [1024], P('pts'), may hold values from 0.5 to 2
- cheb_coef: float32 [5], replicated, may hold values from 0.2 to 1
Outputs:
- hess_vec: float32 [4, 1024, 420], P(None, 'pts')
The draws below stay inside these ranges and needn't reach their ends.
Inputs may be any that keep to these rules, and one draw needn't show every extreme that they name: `offsets`: each point's stencil neighbours lie at most 32 points away in the point order.
All inputs are finite; a program needn't handle non-finite values.
Results may differ from the reference program's by a relative error of at most 0.00016.
Values sent between devices are 32-bit elements; how exact they have to be, the bound alone decides.
No kernel may reach another device: no remote copies, remote signals or barrier semaphores. Data moves between devices by JAX's collectives and lax.ppermute only.
A program may use at most 64 MiB of HBM per device.

```python
import math
import jax
import jax.numpy as jnp
from jax import lax

NT = 420
NV = 4
DEG = 4
NB = 6
PTS_DEV = 32
PTS = 1024
SENSORS = 512
NFP = 448


def place_ends(values, key, smallest, largest):
    shape = values.shape
    index_at = [jax.random.randint(jax.random.fold_in(key, axis), (), 0, shape[axis]) for axis in range(len(shape))]
    values = values.at[tuple(index_at)].set(smallest)
    longest = shape.index(max(shape))
    index_at[longest] = (index_at[longest] + 1) % shape[longest]
    return values.at[tuple(index_at)].set(largest)


def block_levels(rng, extent, cuts, smallest, high):
    def one(axis_at, parts):
        draws = jax.random.uniform(jax.random.fold_in(jax.random.fold_in(rng, 6), axis_at), (parts,), jnp.float32, smallest / len(cuts), high / len(cuts))
        return jnp.repeat(jnp.exp(draws), extent[axis_at] // parts).reshape((-1,) + (1,) * (len(extent) - axis_at - 1))

    factor_of = one(*cuts[0])
    for cut in cuts[1:]:
        factor_of = factor_of * one(*cut)
    return factor_of


def scatter_about(key, extent, scale, bound, cuts=(), kind=jnp.bfloat16):
    level = block_levels(key, extent, cuts, -0.22, 0.18) if cuts else 1.0
    entries = jax.random.normal(key, extent, jnp.float32) * scale * level
    return jnp.minimum(jnp.maximum(entries, -bound), bound).astype(kind)


def setup_inputs(seed: int = 0) -> dict:
    keys = jax.random.split(jax.random.key(seed), 8)
    vectors = scatter_about(keys[0], (NV, PTS, NT), 1.0, 6.0, ((1, 32),), jnp.float32)
    kernel_hat = scatter_about(keys[1], (2, NFP, SENSORS, PTS), PTS ** -0.5, 0.1875, ((1, 32), (2, 8)), jnp.float32)
    noise_prec = jnp.clip(jnp.exp(math.log(3.0) - 2.3025851 * jax.random.uniform(keys[2], (SENSORS,), jnp.float32) ** block_levels(keys[2], (SENSORS,), ((0, 256),), -0.2, 0.2)), 0.3, 3.0)
    stencil_coefficients_raw = jnp.clip(jnp.exp(math.log(2.0) - 2.9957323 * jax.random.uniform(keys[3], (PTS, NB), jnp.float32) ** block_levels(keys[3], (PTS, NB), ((0, 32),), -0.2, 0.2)), 0.1, 2.0)
    offsets = place_ends(jax.random.randint(keys[4], (PTS, NB), 0 - PTS_DEV, PTS_DEV + 1), jax.random.fold_in(keys[4], 1), 0 - PTS_DEV, PTS_DEV).astype(jnp.int32)
    amplitude = jnp.clip(jnp.exp(math.log(2.0) - 1.3862944 * jax.random.uniform(keys[5], (PTS,), jnp.float32) ** block_levels(keys[5], (PTS,), ((0, 32),), -0.2, 0.2)), 0.5, 2.0)
    cheb_coef = jnp.clip(jnp.exp(jax.random.uniform(keys[6], (DEG + 1,), jnp.float32, math.log(0.2), math.log(1.0))), 0.2, 1.0)
    return dict(vectors=vectors, kernel_hat=kernel_hat, noise_prec=noise_prec, stencil_coefficients_raw=stencil_coefficients_raw, offsets=offsets, amplitude=amplitude, cheb_coef=cheb_coef)


def stencil_parts(point_count, stencil_coefficients_raw, offsets):
    weights = stencil_coefficients_raw / jnp.sum(stencil_coefficients_raw, axis=1, keepdims=True)
    target = jnp.arange(point_count, dtype=jnp.int32)[:, None] + offsets
    inside = (target >= 0) & (target < point_count)
    weights = jnp.where(inside, weights, jnp.zeros_like(weights))
    clipped = jnp.clip(target, 0, point_count - 1).astype(jnp.int32)
    return weights, clipped


def chebyshev(values_in, operator, cheb_coef):
    previous = values_in
    current = operator(values_in)
    running_sum = cheb_coef[0] * previous + cheb_coef[1] * current
    for degree in range(2, DEG + 1):
        following = 2.0 * operator(current) - previous
        previous, current = current, following
        running_sum = running_sum + cheb_coef[degree] * current
    return running_sum


def prior_operator_apply(values_in, stencil_coefficients_raw, offsets, amplitude, cheb_coef):
    weights, clipped = stencil_parts(values_in.shape[1], stencil_coefficients_raw, offsets)

    def neighbour_mean(values):
        picked = jnp.take(values, clipped, axis=1)
        return jnp.sum(weights[None, :, :, None] * picked, axis=2)

    return amplitude[None, :, None] * chebyshev(values_in, neighbour_mean, cheb_coef)


def apply_prior_transposed(values_in, stencil_coefficients_raw, offsets, amplitude, cheb_coef):
    weights, clipped = stencil_parts(values_in.shape[1], stencil_coefficients_raw, offsets)

    def spread_back(values):
        contrib = weights[None, :, :, None] * values[:, :, None, :]
        return jnp.zeros_like(values).at[:, clipped].add(contrib)

    return chebyshev(amplitude[None, :, None] * values_in, spread_back, cheb_coef)


def reference(vectors, kernel_hat, noise_prec, stencil_coefficients_raw, offsets, amplitude, cheb_coef):
    exact_evaluation_flag = lax.Precision.HIGHEST
    frequency_total_count = NT + 1
    prior_field = prior_operator_apply(vectors, stencil_coefficients_raw, offsets, amplitude, cheb_coef)
    spectrum = jnp.fft.rfft(prior_field, n=2 * NT, axis=2)
    spectrum_real = jnp.transpose(spectrum.real, (2, 0, 1))
    spectrum_imag = jnp.transpose(spectrum.imag, (2, 0, 1))
    freq_index = jnp.arange(frequency_total_count, dtype=jnp.int32)

    def forward_one(items):
        index_now, real_part, imag_part = items
        kernel_rows = lax.dynamic_index_in_dim(kernel_hat, index_now, 1, keepdims=False)
        kernel_real, kernel_imag = kernel_rows[0], kernel_rows[1]
        data_real = jnp.dot(real_part, kernel_real.T, precision=exact_evaluation_flag) - jnp.dot(imag_part, kernel_imag.T, precision=exact_evaluation_flag)
        data_imag = jnp.dot(imag_part, kernel_real.T, precision=exact_evaluation_flag) + jnp.dot(real_part, kernel_imag.T, precision=exact_evaluation_flag)
        return data_real, data_imag

    data_real, data_imag = lax.map(forward_one, (freq_index, spectrum_real, spectrum_imag))
    data_spec = jnp.transpose(data_real, (1, 2, 0)) + 1j * jnp.transpose(data_imag, (1, 2, 0))
    data = jnp.fft.irfft(data_spec, n=2 * NT, axis=2)[:, :, :NT] * noise_prec[None, :, None]
    data_back = jnp.fft.rfft(data, n=2 * NT, axis=2)
    back_real = jnp.transpose(data_back.real, (2, 0, 1))
    back_imag = jnp.transpose(data_back.imag, (2, 0, 1))

    def adjoint_one(items):
        index_now, real_part, imag_part = items
        kernel_rows = lax.dynamic_index_in_dim(kernel_hat, index_now, 1, keepdims=False)
        kernel_real, kernel_imag = kernel_rows[0], kernel_rows[1]
        grad_real = jnp.dot(real_part, kernel_real, precision=exact_evaluation_flag) + jnp.dot(imag_part, kernel_imag, precision=exact_evaluation_flag)
        grad_imag = jnp.dot(imag_part, kernel_real, precision=exact_evaluation_flag) - jnp.dot(real_part, kernel_imag, precision=exact_evaluation_flag)
        return grad_real, grad_imag

    grad_real, grad_imag = lax.map(adjoint_one, (freq_index, back_real, back_imag))
    grad_spec = jnp.transpose(grad_real, (1, 2, 0)) + 1j * jnp.transpose(grad_imag, (1, 2, 0))
    gradient = jnp.fft.irfft(grad_spec, n=2 * NT, axis=2)[:, :, :NT]
    return vectors + apply_prior_transposed(gradient, stencil_coefficients_raw, offsets, amplitude, cheb_coef)
```

```python
import numpy as np
import jax
import jax.numpy as jnp
from jax import lax
from jax.experimental import pallas as pl
from jax.experimental.pallas import tpu as pltpu
from jax.sharding import PartitionSpec as P

LANES = 128
SPAN = 256
REACH = 64
SLOTS = 16


def spare_lane(item):
    return 32 * (item // 4) + 28 + item % 4


def halves(values):
    high = values.astype(jnp.bfloat16)
    low = (values - high.astype(jnp.float32)).astype(jnp.bfloat16)
    return high, low


def host_halves(values):
    values = values.astype(np.float32)
    high = values.astype(jnp.bfloat16)
    low = (values - high.astype(np.float32)).astype(jnp.bfloat16)
    return high, low


def tables(length, block, blocks, padded_time):
    time = np.arange(length)

    def angle(frequency):
        return np.pi / length * ((frequency[:, None] * time[None, :]) % (2 * length))

    base = angle(np.arange(blocks) * block)
    coarse = np.zeros((blocks, 2, padded_time))
    coarse[:, 0, :length] = np.cos(base)
    coarse[:, 1, :length] = np.sin(base)
    coarse = coarse.reshape(blocks, 2 * padded_time)
    fine_angle = angle(np.arange(block))
    fine = np.zeros((2, SLOTS, 2, padded_time))
    fine[0, :block, 0, :length] = np.cos(fine_angle)
    fine[0, :block, 1, :length] = -np.sin(fine_angle)
    fine[1, :block, 0, :length] = -np.sin(fine_angle)
    fine[1, :block, 1, :length] = -np.cos(fine_angle)
    fine = fine.reshape(2, 2 * SLOTS, padded_time)
    full_angle = angle(np.arange(blocks * block)).reshape(blocks, block, length)
    full = np.zeros((padded_time, blocks, SLOTS, 2))
    full[:length, :, :block, 0] = np.cos(full_angle).transpose(2, 0, 1)
    full[:length, :, :block, 1] = -np.sin(full_angle).transpose(2, 0, 1)
    full = full.reshape(padded_time, blocks * 2 * SLOTS)
    coarse_high, coarse_low = host_halves(coarse)
    to_time = np.concatenate([coarse_high, coarse_high, coarse_low, coarse_low], axis=0)
    to_frequency = np.concatenate([coarse_high, coarse_low], axis=0).T.copy()
    full_high, full_low = host_halves(full)
    return full_high, full_low, to_time, to_frequency, fine.astype(np.float32)


def dot(a, b):
    return jnp.dot(a, b, preferred_element_type=jnp.float32)


def iota(shape, axis):
    return lax.broadcasted_iota(jnp.int32, shape, axis)


def source_kernel(vectors, raw, offsets, amplitude, full_high, full_low, out, padded, items):
    count, points, length = vectors.shape
    padded[...] = jnp.zeros_like(padded)
    for v in range(count):
        padded[v * points : (v + 1) * points, :length] = vectors[v]
    items[...] = jnp.zeros_like(items)
    near = raw.shape[0]
    weights = raw[...] / jnp.sum(raw[...], axis=0, keepdims=True)
    shifts = offsets[...].astype(jnp.float32)
    for k in range(near):
        lane = spare_lane(k)
        items[lane : lane + 1, :points] = weights[k : k + 1]
        lane = spare_lane(near + k)
        items[lane : lane + 1, :points] = shifts[k : k + 1]
    lane = spare_lane(2 * near)
    items[lane : lane + 1, :points] = amplitude[...]
    extra = items[...].T[:points]
    rows = count * points
    high, low = halves(padded[...])
    both = jnp.concatenate([high, low], axis=0)
    group_of_lane = iota((points, LANES), 1) // 32
    width = SPAN
    for start in range(0, full_high.shape[1], width):
        first = dot(both, full_high[:, start : start + width])
        second = dot(high, full_low[:, start : start + width])
        spectrum = first[:rows] + first[rows:] + second
        for tile in range(width // LANES):
            part = spectrum[:, tile * LANES : (tile + 1) * LANES]
            for e in range(4):
                block = extra
                for v in range(count):
                    piece = part[v * points : (v + 1) * points]
                    shift = (32 * (v - e)) % LANES
                    if shift:
                        piece = pltpu.roll(piece, shift, 1)
                    block = block + jnp.where(group_of_lane == v, piece, 0.0)
                out[start // 32 + tile * 4 + e] = block


def chebyshev(load, store, band, coef, previous, current, total, state):
    points = total.shape[0]
    rows = LANES
    blocks = points // rows
    edge = jnp.zeros((REACH, SPAN), jnp.bfloat16)
    for parity in range(2):
        state[parity, :REACH] = edge
        state[parity, REACH + points :] = edge

    def put(parity, b, values):
        high, low = halves(values)
        state[parity, REACH + b * rows : REACH + (b + 1) * rows, :LANES] = high
        state[parity, REACH + b * rows : REACH + (b + 1) * rows, LANES:] = low

    for b in range(blocks):
        at = slice(b * rows, (b + 1) * rows)
        values = load(b)
        previous[at] = values
        total[at] = coef[0] * values
        put(0, b, values)
    degree = coef.shape[0] - 1
    for j in range(1, degree + 1):
        for b in range(blocks):
            at = slice(b * rows, (b + 1) * rows)
            product = dot(band[b], state[(j - 1) % 2, b * rows : b * rows + SPAN])
            moved = product[:rows, :LANES] + product[:rows, LANES:] + product[rows:, :LANES]
            if j == 1:
                values = moved
            else:
                values = 2.0 * moved - previous[at]
                if j < degree:
                    previous[at] = current[at]
            if j < degree:
                current[at] = values
                total[at] = total[at] + coef[j] * values
                put(j % 2, b, values)
            else:
                store(b, total[at] + coef[j] * values)


def put_band(band, b, matrix):
    high, low = halves(matrix)
    band[b, :LANES] = high
    band[b, LANES:] = low


def item(table, index):
    lane = spare_lane(index)
    return table[:, lane : lane + 1]


def lane_frequency(shape):
    return (iota(shape, 1) % 32) // 2


def swapped(values):
    real = iota(values.shape, 1) % 2 == 0
    following = pltpu.roll(values, LANES - 1, 1)
    leading = pltpu.roll(values, 1, 1)
    return real, following, leading


def forward_kernel(near, received, coef, kernel, out, band, previous, current, total, state, ready, held, sems):
    pairs = sems.shape[0]
    copies = []
    for g in range(pairs):
        copy = pltpu.make_async_copy(kernel.at[:, pl.ds(2 * g, 2)], held.at[:, pl.ds(2 * g, 2)], sems.at[g])
        copy.start()
        copies.append(copy)
    points = total.shape[0]
    column = iota((LANES, SPAN), 1).astype(jnp.float32)
    row = iota((LANES, 1), 0).astype(jnp.float32)
    for b in range(points // LANES):
        table = received[b * LANES : (b + 1) * LANES]
        matrix = jnp.zeros((LANES, SPAN), jnp.float32)
        for k in range(near):
            target = item(table, near + k) + (row + float(REACH))
            matrix = matrix + jnp.where(column == target, item(table, k), 0.0)
        put_band(band, b, matrix)

    def load(b):
        return received[b * LANES : (b + 1) * LANES]

    def store(b, values):
        at = slice(b * LANES, (b + 1) * LANES)
        high, low = halves(item(received[at], 2 * near) * values)
        ready[at, :LANES] = high
        ready[at, LANES:] = low

    chebyshev(load, store, band, coef, previous, current, total, state)
    sensors = out.shape[0]
    of_lane = lane_frequency((sensors, LANES))
    direct = jnp.zeros((sensors, LANES), jnp.float32)
    crossed = jnp.zeros((sensors, LANES), jnp.float32)
    for g in range(pairs):
        copies[g].wait()
        parts = []
        for f in (2 * g, 2 * g + 1):
            for c in range(2):
                parts.extend(halves(held[c, f]))
        product = dot(jnp.concatenate(parts, axis=0), ready[...])
        for n, f in enumerate((2 * g, 2 * g + 1)):
            sums = []
            for c in range(2):
                at = (2 * n + c) * 2 * sensors
                top = product[at : at + sensors]
                bottom = product[at + sensors : at + 2 * sensors]
                sums.append(top[:, :LANES] + top[:, LANES:] + bottom[:, :LANES])
            direct = jnp.where(of_lane == f, sums[0], direct)
            crossed = jnp.where(of_lane == f, sums[1], crossed)
    real, following, leading = swapped(crossed)
    out[...] = direct + jnp.where(real, -following, leading)


def frequency_weight(block, blocks, length):
    shape = (blocks, LANES)
    slot = lane_frequency(shape)
    frequency = iota(shape, 0) * block + slot
    edge = (frequency == 0) | (frequency == length)
    weight = jnp.where(edge, 0.5 / length, 1.0 / length).astype(jnp.float32)
    return jnp.where((slot < block) & (frequency <= length), weight, 0.0)


def series(received, sets, blocks, weight, to_time, fine, each):
    padded_time = fine.shape[2]
    stacked = []
    for n in range(sets):
        values = received[pl.ds(n, blocks, stride=sets), :] * weight
        high = values.astype(jnp.bfloat16).astype(jnp.float32)
        low = values - high
        stacked.append(jnp.concatenate([high, low, high, low], axis=0).T.astype(jnp.bfloat16))
    product = dot(jnp.concatenate(stacked, axis=0), to_time[...])
    for n in range(sets):
        for v in range(4):
            at = n * LANES + v * 32
            rows = product[at : at + 32]
            terms = rows[:, :padded_time] * fine[0] + rows[:, padded_time:] * fine[1]
            each(n, v, jnp.sum(terms, axis=0, keepdims=True))


def sensor_kernel(block, length, received, noise, to_time, to_frequency, fine, out, moved):
    blocks = out.shape[0] // 2
    padded_time = fine.shape[2]
    weight = frequency_weight(block, blocks, length)

    def each(n, v, values):
        weighted = values * noise[n]
        for half in range(2):
            high, low = halves(weighted * fine[half])
            at = slice(half * padded_time, (half + 1) * padded_time)
            moved[n * SPAN + v * 32 : n * SPAN + v * 32 + 32, at] = high
            moved[n * SPAN + LANES + v * 32 : n * SPAN + LANES + v * 32 + 32, at] = low

    series(received, 2, blocks, weight, to_time, fine, each)
    product = dot(moved[...], to_frequency[...])
    for n in range(2):
        high = product[n * SPAN : n * SPAN + LANES]
        low = product[n * SPAN + LANES : (n + 1) * SPAN]
        result = high[:, :blocks] + high[:, blocks:] + low[:, :blocks]
        out[pl.ds(n, blocks, stride=2), :] = result.T


def adjoint_kernel(near, received, table, coef, kernel, out, band, previous, current, total, state, flat, held, stencil, sems):
    chunks = sems.shape[0]
    copies = []
    for n in range(chunks):
        at = pl.ds(n * SPAN, SPAN)
        copy = pltpu.make_async_copy(kernel.at[:, :, :, at], held.at[:, :, :, at], sems.at[n])
        copy.start()
        copies.append(copy)
    points = total.shape[0]
    blocks = points // LANES
    stencil[...] = jnp.zeros_like(stencil)
    for b in range(blocks):
        turned = table[b * LANES : (b + 1) * LANES].T
        for m in range(2 * near):
            lane = spare_lane(m)
            stencil[m : m + 1, (b + 1) * LANES : (b + 2) * LANES] = turned[lane : lane + 1]
    row = iota((LANES, SPAN), 0).astype(jnp.float32)
    column = iota((1, SPAN), 1).astype(jnp.float32) - float(REACH)
    for b in range(blocks):
        window = pltpu.roll(stencil[:, b * LANES : (b + 3) * LANES], 3 * LANES - REACH, 1)[:, :SPAN]
        matrix = jnp.zeros((LANES, SPAN), jnp.float32)
        for k in range(near):
            target = window[near + k : near + k + 1] + column
            matrix = matrix + jnp.where(row == target, window[k : k + 1], 0.0)
        put_band(band, b, matrix)
    sensors = received.shape[0]
    values = received[...]
    real, following, leading = swapped(values)
    turned = jnp.concatenate([values, jnp.where(real, following, -leading)], axis=0).T
    high, low = halves(turned)
    both = jnp.concatenate([high, low], axis=0)
    of_row = ((iota((2 * LANES, LANES), 0) % 32) // 2)
    frequencies = kernel.shape[1]
    spread = jnp.concatenate(
        [jnp.where(of_row == f, both, jnp.zeros_like(both)) for f in range(frequencies)], axis=1
    )
    for n in range(chunks):
        copies[n].wait()
        highs, lows = [], []
        for f in range(frequencies):
            for c in range(2):
                a, b = halves(held[c, f, :, n * SPAN : (n + 1) * SPAN])
                highs.append(a)
                lows.append(b)
        first = dot(spread, jnp.concatenate(highs, axis=0))
        second = dot(spread[:LANES], jnp.concatenate(lows, axis=0))
        flat[n * SPAN : (n + 1) * SPAN] = (first[:LANES] + first[LANES:] + second).T

    def load(b):
        at = slice(b * LANES, (b + 1) * LANES)
        return item(table[at], 2 * near) * flat[at]

    def store(b, values):
        for i in range(4):
            for j in range(8):
                at = 16 * b + 4 * i
                out[j, at : at + 4] = values[32 * i + 4 * j : 32 * i + 4 * j + 4]

    chebyshev(load, store, band, coef, previous, current, total, state)


def gradient_kernel(block, length, received, to_time, fine, out, once):
    blocks = received.shape[0] // 4
    weight = frequency_weight(block, blocks, length)

    def each(n, v, values):
        for tile in range(values.shape[1] // LANES):
            at = 16 * tile + 4 * v + n
            once[at : at + 1] = values[:, tile * LANES : (tile + 1) * LANES]

    series(received, 4, blocks, weight, to_time, fine, each)
    for copy in range(out.shape[0]):
        out[copy] = once[...]


def final_kernel(received, vectors, out):
    count, _, length = out.shape
    groups = received.shape[0]
    for tile in range(received.shape[1] // 16):
        lanes = min(LANES, length - tile * LANES)
        at = slice(tile * LANES, tile * LANES + lanes)
        for v in range(count):
            rows = [received[j, 16 * tile + 4 * v : 16 * tile + 4 * v + 4] for j in range(groups)]
            out[v, :, at] = vectors[v, :, at] + jnp.concatenate(rows, axis=0)[:, :lanes]


VMEM = pl.BlockSpec(memory_space=pltpu.VMEM)
SMEM = pl.BlockSpec(memory_space=pltpu.SMEM)
ANY = pl.BlockSpec(memory_space=pl.ANY)


def call(kernel, name, shape, specs, scratch=()):
    return pl.pallas_call(
        kernel,
        name=name,
        out_shape=jax.ShapeDtypeStruct(shape, jnp.float32),
        in_specs=specs,
        out_specs=VMEM,
        scratch_shapes=list(scratch),
    )


def exchange(values, axis):
    return lax.all_to_all(values, axis, 0, 0, tiled=True)


def body(vectors, kernel_hat, noise_prec, stencil_coefficients_raw, offsets, amplitude, cheb_coef):
    from functools import partial

    count, points, length = vectors.shape
    _, block, sensors, all_points = kernel_hat.shape
    near = offsets.shape[1]
    blocks = lax.axis_size("pts")
    groups = lax.axis_size("sens")
    padded_time = 512
    full_high, full_low, to_time, to_frequency, fine = tables(length, block, blocks, padded_time)
    f32, bf16 = jnp.float32, jnp.bfloat16
    grid_scratch = [
        pltpu.VMEM((all_points // LANES, SPAN, SPAN), bf16),
        pltpu.VMEM((all_points, LANES), f32),
        pltpu.VMEM((all_points, LANES), f32),
        pltpu.VMEM((all_points, LANES), f32),
        pltpu.VMEM((2, all_points + 2 * REACH, SPAN), bf16),
    ]
    source = call(
        source_kernel,
        "source",
        (blocks, points, LANES),
        [VMEM] * 6,
        [pltpu.VMEM((count * points, padded_time), f32), pltpu.VMEM((LANES, LANES), f32)],
    )(vectors, stencil_coefficients_raw.T, offsets.T, amplitude.reshape(1, points), full_high, full_low)
    spectrum = exchange(source, "pts").reshape(all_points, LANES)
    data = call(
        partial(forward_kernel, near),
        "forward",
        (sensors, LANES),
        [VMEM, SMEM, ANY],
        grid_scratch
        + [
            pltpu.VMEM((all_points, SPAN), bf16),
            pltpu.VMEM(kernel_hat.shape, f32),
            pltpu.SemaphoreType.DMA((block // 2,)),
        ],
    )(spectrum, cheb_coef, kernel_hat)
    data = exchange(data.reshape(blocks, sensors // blocks, LANES), "pts").reshape(sensors, LANES)
    back = call(
        partial(sensor_kernel, block, length),
        "sensor",
        (sensors, LANES),
        [VMEM, SMEM, VMEM, VMEM, VMEM],
        [pltpu.VMEM((2 * SPAN, 2 * padded_time), bf16)],
    )(data, noise_prec, to_time, to_frequency, fine)
    back = exchange(back.reshape(blocks, sensors // blocks, LANES), "pts").reshape(sensors, LANES)
    partial_sums = call(
        partial(adjoint_kernel, near),
        "adjoint",
        (groups, all_points // groups, LANES),
        [VMEM, VMEM, SMEM, ANY],
        grid_scratch
        + [
            pltpu.VMEM((all_points, LANES), f32),
            pltpu.VMEM(kernel_hat.shape, f32),
            pltpu.VMEM((SLOTS, all_points + 2 * LANES), f32),
            pltpu.SemaphoreType.DMA((all_points // SPAN,)),
        ],
    )(back, spectrum, cheb_coef, kernel_hat)
    summed = jnp.sum(exchange(partial_sums, "sens"), axis=0)
    share = points // groups
    moved = exchange(summed.reshape(blocks, share, LANES), "pts").reshape(blocks * share, LANES)
    gradient = call(
        partial(gradient_kernel, block, length),
        "gradient",
        (groups, share * count * padded_time // LANES, LANES),
        [VMEM, VMEM, VMEM],
        [pltpu.VMEM((share * count * padded_time // LANES, LANES), f32)],
    )(moved, to_time, fine)
    gathered = exchange(gradient, "sens")
    return call(final_kernel, "final", (count, points, length), [VMEM, VMEM])(gathered, vectors)


def solution(mesh):
    placed = (
        P(None, "pts", None),
        P(None, "pts", "sens", None),
        P(("sens", "pts")),
        P("pts", None),
        P("pts", None),
        P("pts"),
        P(),
    )
    return jax.shard_map(
        body, mesh=mesh, in_specs=placed, out_specs=P(None, "pts", None), check_vma=False
    )
```

```python
import numpy as np
import jax
import jax.numpy as jnp
from jax import lax
from jax.experimental import pallas as pl
from jax.experimental.pallas import tpu as pltpu
from jax.sharding import PartitionSpec as P

LANES = 128
SPAN = 256
REACH = 64
SLOTS = 16


def spare_lane(item):
    return 32 * (item // 4) + 28 + item % 4


def halves(values):
    high = values.astype(jnp.bfloat16)
    low = (values - high.astype(jnp.float32)).astype(jnp.bfloat16)
    return high, low


def host_halves(values):
    values = values.astype(np.float32)
    high = values.astype(jnp.bfloat16)
    low = (values - high.astype(np.float32)).astype(jnp.bfloat16)
    return high, low


def tables(length, block, blocks, padded_time):
    time = np.arange(length)

    def angle(frequency):
        return np.pi / length * ((frequency[:, None] * time[None, :]) % (2 * length))

    base = angle(np.arange(blocks) * block)
    coarse = np.zeros((blocks, 2, padded_time))
    coarse[:, 0, :length] = np.cos(base)
    coarse[:, 1, :length] = np.sin(base)
    coarse = coarse.reshape(blocks, 2 * padded_time)
    fine_angle = angle(np.arange(block))
    fine = np.zeros((2, SLOTS, 2, padded_time))
    fine[0, :block, 0, :length] = np.cos(fine_angle)
    fine[0, :block, 1, :length] = -np.sin(fine_angle)
    fine[1, :block, 0, :length] = -np.sin(fine_angle)
    fine[1, :block, 1, :length] = -np.cos(fine_angle)
    fine = fine.reshape(2, 2 * SLOTS, padded_time)
    full_angle = angle(np.arange(blocks * block)).reshape(blocks, block, length)
    full = np.zeros((padded_time, blocks, SLOTS, 2))
    full[:length, :, :block, 0] = np.cos(full_angle).transpose(2, 0, 1)
    full[:length, :, :block, 1] = -np.sin(full_angle).transpose(2, 0, 1)
    full = full.reshape(padded_time, blocks * 2 * SLOTS)
    coarse_high, coarse_low = host_halves(coarse)
    to_time = np.concatenate([coarse_high, coarse_high, coarse_low, coarse_low], axis=0)
    to_frequency = np.concatenate([coarse_high, coarse_low], axis=0).T.copy()
    full_high, full_low = host_halves(full)
    return full_high, full_low, to_time, to_frequency, fine.astype(np.float32)


def dot(a, b):
    return jnp.dot(a, b, preferred_element_type=jnp.float32)


def iota(shape, axis):
    return lax.broadcasted_iota(jnp.int32, shape, axis)


def source_kernel(vectors, raw, offsets, amplitude, full_high, full_low, out, padded, items):
    count, points, length = vectors.shape
    padded[...] = jnp.zeros_like(padded)
    for v in range(count):
        padded[v * points : (v + 1) * points, :length] = vectors[v]
    items[...] = jnp.zeros_like(items)
    near = raw.shape[0]
    weights = raw[...] / jnp.sum(raw[...], axis=0, keepdims=True)
    shifts = offsets[...].astype(jnp.float32)
    for k in range(near):
        lane = spare_lane(k)
        items[lane : lane + 1, :points] = weights[k : k + 1]
        lane = spare_lane(near + k)
        items[lane : lane + 1, :points] = shifts[k : k + 1]
    lane = spare_lane(2 * near)
    items[lane : lane + 1, :points] = amplitude[...]
    extra = items[...].T[:points]
    rows = count * points
    high, low = halves(padded[...])
    both = jnp.concatenate([high, low], axis=0)
    group_of_lane = iota((points, LANES), 1) // 32
    width = SPAN
    for start in range(0, full_high.shape[1], width):
        first = dot(both, full_high[:, start : start + width])
        second = dot(high, full_low[:, start : start + width])
        spectrum = first[:rows] + first[rows:] + second
        for tile in range(width // LANES):
            part = spectrum[:, tile * LANES : (tile + 1) * LANES]
            for e in range(4):
                block = extra
                for v in range(count):
                    piece = part[v * points : (v + 1) * points]
                    shift = (32 * (v - e)) % LANES
                    if shift:
                        piece = pltpu.roll(piece, shift, 1)
                    block = block + jnp.where(group_of_lane == v, piece, 0.0)
                out[start // 32 + tile * 4 + e] = block


def chebyshev(load, store, band, coef, previous, current, total, state):
    points = total.shape[0]
    rows = LANES
    blocks = points // rows
    edge = jnp.zeros((REACH, SPAN), jnp.bfloat16)
    for parity in range(2):
        state[parity, :REACH] = edge
        state[parity, REACH + points :] = edge

    def put(parity, b, values):
        high, low = halves(values)
        state[parity, REACH + b * rows : REACH + (b + 1) * rows, :LANES] = high
        state[parity, REACH + b * rows : REACH + (b + 1) * rows, LANES:] = low

    for b in range(blocks):
        at = slice(b * rows, (b + 1) * rows)
        values = load(b)
        previous[at] = values
        total[at] = coef[0] * values
        put(0, b, values)
    degree = coef.shape[0] - 1
    for j in range(1, degree + 1):
        for b in range(blocks):
            at = slice(b * rows, (b + 1) * rows)
            product = dot(band[b], state[(j - 1) % 2, b * rows : b * rows + SPAN])
            moved = product[:rows, :LANES] + product[:rows, LANES:] + product[rows:, :LANES]
            if j == 1:
                values = moved
            else:
                values = 2.0 * moved - previous[at]
                if j < degree:
                    previous[at] = current[at]
            if j < degree:
                current[at] = values
                total[at] = total[at] + coef[j] * values
                put(j % 2, b, values)
            else:
                store(b, total[at] + coef[j] * values)


def put_band(band, b, matrix):
    high, low = halves(matrix)
    band[b, :LANES] = high
    band[b, LANES:] = low


def item(table, index):
    lane = spare_lane(index)
    return table[:, lane : lane + 1]


def lane_frequency(shape):
    return (iota(shape, 1) % 32) // 2


def swapped(values):
    real = iota(values.shape, 1) % 2 == 0
    following = pltpu.roll(values, LANES - 1, 1)
    leading = pltpu.roll(values, 1, 1)
    return real, following, leading


def forward_kernel(
    near, received, coef, kernel, out, highs, lows, band, previous, current, total, state, ready, held, sems
):
    pairs = sems.shape[0]
    copies = []
    for g in range(pairs):
        copy = pltpu.make_async_copy(kernel.at[:, pl.ds(2 * g, 2)], held.at[:, pl.ds(2 * g, 2)], sems.at[g])
        copy.start()
        copies.append(copy)
    points = total.shape[0]
    column = iota((LANES, SPAN), 1).astype(jnp.float32)
    row = iota((LANES, 1), 0).astype(jnp.float32)
    for b in range(points // LANES):
        table = received[b * LANES : (b + 1) * LANES]
        matrix = jnp.zeros((LANES, SPAN), jnp.float32)
        for k in range(near):
            target = item(table, near + k) + (row + float(REACH))
            matrix = matrix + jnp.where(column == target, item(table, k), 0.0)
        put_band(band, b, matrix)

    def load(b):
        return received[b * LANES : (b + 1) * LANES]

    def store(b, values):
        at = slice(b * LANES, (b + 1) * LANES)
        high, low = halves(item(received[at], 2 * near) * values)
        ready[at, :LANES] = high
        ready[at, LANES:] = low

    chebyshev(load, store, band, coef, previous, current, total, state)
    sensors = out.shape[0]
    of_lane = lane_frequency((sensors, LANES))
    direct = jnp.zeros((sensors, LANES), jnp.float32)
    crossed = jnp.zeros((sensors, LANES), jnp.float32)
    for g in range(pairs):
        copies[g].wait()
        parts = []
        for f in (2 * g, 2 * g + 1):
            for c in range(2):
                high, low = halves(held[c, f])
                highs[c, f] = high
                lows[c, f] = low
                parts.extend((high, low))
        product = dot(jnp.concatenate(parts, axis=0), ready[...])
        for n, f in enumerate((2 * g, 2 * g + 1)):
            sums = []
            for c in range(2):
                at = (2 * n + c) * 2 * sensors
                top = product[at : at + sensors]
                bottom = product[at + sensors : at + 2 * sensors]
                sums.append(top[:, :LANES] + top[:, LANES:] + bottom[:, :LANES])
            direct = jnp.where(of_lane == f, sums[0], direct)
            crossed = jnp.where(of_lane == f, sums[1], crossed)
    real, following, leading = swapped(crossed)
    out[...] = direct + jnp.where(real, -following, leading)


def frequency_weight(block, blocks, length):
    shape = (blocks, LANES)
    slot = lane_frequency(shape)
    frequency = iota(shape, 0) * block + slot
    edge = (frequency == 0) | (frequency == length)
    weight = jnp.where(edge, 0.5 / length, 1.0 / length).astype(jnp.float32)
    return jnp.where((slot < block) & (frequency <= length), weight, 0.0)


def series(received, sets, blocks, weight, to_time, fine, each):
    padded_time = fine.shape[2]
    stacked = []
    for n in range(sets):
        values = received[pl.ds(n, blocks, stride=sets), :] * weight
        high = values.astype(jnp.bfloat16).astype(jnp.float32)
        low = values - high
        stacked.append(jnp.concatenate([high, low, high, low], axis=0).T.astype(jnp.bfloat16))
    product = dot(jnp.concatenate(stacked, axis=0), to_time[...])
    for n in range(sets):
        for v in range(4):
            at = n * LANES + v * 32
            rows = product[at : at + 32]
            terms = rows[:, :padded_time] * fine[0] + rows[:, padded_time:] * fine[1]
            each(n, v, jnp.sum(terms, axis=0, keepdims=True))


def sensor_kernel(block, length, received, noise, to_time, to_frequency, fine, out, moved):
    blocks = out.shape[0] // 2
    padded_time = fine.shape[2]
    weight = frequency_weight(block, blocks, length)

    def each(n, v, values):
        weighted = values * noise[n]
        for half in range(2):
            high, low = halves(weighted * fine[half])
            at = slice(half * padded_time, (half + 1) * padded_time)
            moved[n * SPAN + v * 32 : n * SPAN + v * 32 + 32, at] = high
            moved[n * SPAN + LANES + v * 32 : n * SPAN + LANES + v * 32 + 32, at] = low

    series(received, 2, blocks, weight, to_time, fine, each)
    product = dot(moved[...], to_frequency[...])
    for n in range(2):
        high = product[n * SPAN : n * SPAN + LANES]
        low = product[n * SPAN + LANES : (n + 1) * SPAN]
        result = high[:, :blocks] + high[:, blocks:] + low[:, :blocks]
        out[pl.ds(n, blocks, stride=2), :] = result.T


def adjoint_kernel(near, received, table, coef, highs, lows, out, band, previous, current, total, state, flat, stencil):
    chunks = highs.shape[3] // SPAN
    frequencies = highs.shape[1]
    points = total.shape[0]
    blocks = points // LANES
    stencil[...] = jnp.zeros_like(stencil)
    for b in range(blocks):
        turned = table[b * LANES : (b + 1) * LANES].T
        for m in range(2 * near):
            lane = spare_lane(m)
            stencil[m : m + 1, (b + 1) * LANES : (b + 2) * LANES] = turned[lane : lane + 1]
    row = iota((LANES, SPAN), 0).astype(jnp.float32)
    column = iota((1, SPAN), 1).astype(jnp.float32) - float(REACH)
    for b in range(blocks):
        window = pltpu.roll(stencil[:, b * LANES : (b + 3) * LANES], 3 * LANES - REACH, 1)[:, :SPAN]
        matrix = jnp.zeros((LANES, SPAN), jnp.float32)
        for k in range(near):
            target = window[near + k : near + k + 1] + column
            matrix = matrix + jnp.where(row == target, window[k : k + 1], 0.0)
        put_band(band, b, matrix)
    sensors = received.shape[0]
    values = received[...]
    real, following, leading = swapped(values)
    turned = jnp.concatenate([values, jnp.where(real, following, -leading)], axis=0).T
    high, low = halves(turned)
    both = jnp.concatenate([high, low], axis=0)
    of_row = ((iota((2 * LANES, LANES), 0) % 32) // 2)
    spread = jnp.concatenate(
        [jnp.where(of_row == f, both, jnp.zeros_like(both)) for f in range(frequencies)], axis=1
    )
    for n in range(chunks):
        at = slice(n * SPAN, (n + 1) * SPAN)
        order = [(c, f) for f in range(frequencies) for c in range(2)]
        first = dot(spread, jnp.concatenate([highs[c, f, :, at] for c, f in order], axis=0))
        second = dot(spread[:LANES], jnp.concatenate([lows[c, f, :, at] for c, f in order], axis=0))
        flat[n * SPAN : (n + 1) * SPAN] = (first[:LANES] + first[LANES:] + second).T

    def load(b):
        at = slice(b * LANES, (b + 1) * LANES)
        return item(table[at], 2 * near) * flat[at]

    def store(b, values):
        for i in range(4):
            for j in range(8):
                at = 16 * b + 4 * i
                out[j, at : at + 4] = values[32 * i + 4 * j : 32 * i + 4 * j + 4]

    chebyshev(load, store, band, coef, previous, current, total, state)


def gradient_kernel(block, length, received, to_time, fine, out, once):
    blocks = received.shape[0] // 4
    weight = frequency_weight(block, blocks, length)

    def each(n, v, values):
        for tile in range(values.shape[1] // LANES):
            at = 16 * tile + 4 * v + n
            once[at : at + 1] = values[:, tile * LANES : (tile + 1) * LANES]

    series(received, 4, blocks, weight, to_time, fine, each)
    for copy in range(out.shape[0]):
        out[copy] = once[...]


def final_kernel(received, vectors, out):
    count, _, length = out.shape
    groups = received.shape[0]
    for tile in range(received.shape[1] // 16):
        lanes = min(LANES, length - tile * LANES)
        at = slice(tile * LANES, tile * LANES + lanes)
        for v in range(count):
            rows = [received[j, 16 * tile + 4 * v : 16 * tile + 4 * v + 4] for j in range(groups)]
            out[v, :, at] = vectors[v, :, at] + jnp.concatenate(rows, axis=0)[:, :lanes]


VMEM = pl.BlockSpec(memory_space=pltpu.VMEM)
SMEM = pl.BlockSpec(memory_space=pltpu.SMEM)
HBM = pl.BlockSpec(memory_space=pltpu.HBM)


def call(kernel, name, shapes, specs, scratch=(), fast=True):
    def result(shape, kind):
        return pltpu.VMEM(shape, kind) if fast else jax.ShapeDtypeStruct(shape, kind)

    outs = [result(shape, kind) for shape, kind in shapes]
    return pl.pallas_call(
        kernel,
        name=name,
        out_shape=outs if len(outs) > 1 else outs[0],
        in_specs=specs,
        out_specs=[VMEM] * len(outs) if len(outs) > 1 else VMEM,
        scratch_shapes=list(scratch),
        compiler_params=pltpu.CompilerParams(vmem_limit_bytes=28 * 1024 * 1024),
    )


def exchange(values, axis):
    return lax.all_to_all(values, axis, 0, 0, tiled=True)


def near_core(values):
    return pltpu.with_memory_space_constraint(values, pltpu.VMEM)


def in_place(values):
    return pltpu.with_memory_space_constraint(values, pltpu.HBM)


def body(vectors, kernel_hat, noise_prec, stencil_coefficients_raw, offsets, amplitude, cheb_coef):
    from functools import partial

    count, points, length = vectors.shape
    _, block, sensors, all_points = kernel_hat.shape
    near = offsets.shape[1]
    blocks = lax.axis_size("pts")
    groups = lax.axis_size("sens")
    padded_time = 512
    full_high, full_low, to_time, to_frequency, fine = tables(length, block, blocks, padded_time)
    f32, bf16 = jnp.float32, jnp.bfloat16
    to_time, to_frequency, fine = (near_core(jnp.asarray(table)) for table in (to_time, to_frequency, fine))
    grid_scratch = [
        pltpu.VMEM((all_points // LANES, SPAN, SPAN), bf16),
        pltpu.VMEM((all_points, LANES), f32),
        pltpu.VMEM((all_points, LANES), f32),
        pltpu.VMEM((all_points, LANES), f32),
        pltpu.VMEM((2, all_points + 2 * REACH, SPAN), bf16),
    ]
    source = call(
        source_kernel,
        "source",
        [((blocks, points, LANES), f32)],
        [VMEM] * 6,
        [pltpu.VMEM((count * points, padded_time), f32), pltpu.VMEM((LANES, LANES), f32)],
    )(
        *map(
            in_place,
            (
                vectors,
                stencil_coefficients_raw.T,
                offsets.T,
                amplitude.reshape(1, points),
                jnp.asarray(full_high),
                jnp.asarray(full_low),
            ),
        )
    )
    spectrum = near_core(exchange(source, "pts").reshape(all_points, LANES))
    data, kernel_high, kernel_low = call(
        partial(forward_kernel, near),
        "forward",
        [((sensors, LANES), f32), (kernel_hat.shape, bf16), (kernel_hat.shape, bf16)],
        [VMEM, SMEM, HBM],
        grid_scratch
        + [
            pltpu.VMEM((all_points, SPAN), bf16),
            pltpu.VMEM(kernel_hat.shape, f32),
            pltpu.SemaphoreType.DMA((block // 2,)),
        ],
    )(spectrum, cheb_coef, in_place(kernel_hat))
    data = near_core(exchange(data.reshape(blocks, sensors // blocks, LANES), "pts").reshape(sensors, LANES))
    back = call(
        partial(sensor_kernel, block, length),
        "sensor",
        [((sensors, LANES), f32)],
        [VMEM, SMEM, VMEM, VMEM, VMEM],
        [pltpu.VMEM((2 * SPAN, 2 * padded_time), bf16)],
    )(data, noise_prec, to_time, to_frequency, fine)
    back = near_core(exchange(back.reshape(blocks, sensors // blocks, LANES), "pts").reshape(sensors, LANES))
    partial_sums = call(
        partial(adjoint_kernel, near),
        "adjoint",
        [((groups, all_points // groups, LANES), f32)],
        [VMEM, VMEM, SMEM, VMEM, VMEM],
        grid_scratch
        + [pltpu.VMEM((all_points, LANES), f32), pltpu.VMEM((SLOTS, all_points + 2 * LANES), f32)],
    )(back, spectrum, cheb_coef, near_core(kernel_high), near_core(kernel_low))
    summed = jnp.sum(exchange(partial_sums, "sens"), axis=0)
    share = points // groups
    moved = near_core(exchange(summed.reshape(blocks, share, LANES), "pts").reshape(blocks * share, LANES))
    gradient = call(
        partial(gradient_kernel, block, length),
        "gradient",
        [((groups, share * count * padded_time // LANES, LANES), f32)],
        [VMEM, VMEM, VMEM],
        [pltpu.VMEM((share * count * padded_time // LANES, LANES), f32)],
    )(moved, to_time, fine)
    gathered = near_core(exchange(gradient, "sens"))
    return call(final_kernel, "final", [((count, points, length), f32)], [VMEM, VMEM], fast=False)(gathered, vectors)


def solution(mesh):
    placed = (
        P(None, "pts", None),
        P(None, "pts", "sens", None),
        P(("sens", "pts")),
        P("pts", None),
        P("pts", None),
        P("pts"),
        P(),
    )
    return jax.shard_map(
        body, mesh=mesh, in_specs=placed, out_specs=P(None, "pts", None), check_vma=False
    )
```

```python
import numpy as np
import jax
import jax.numpy as jnp
from jax import lax
from jax.experimental import pallas as pl
from jax.experimental.pallas import tpu as pltpu
from jax.sharding import PartitionSpec as P

LANES = 128
SPAN = 256
REACH = 64
SLOTS = 16


def spare_lane(item):
    return 32 * (item // 4) + 28 + item % 4


def halves(values):
    high = values.astype(jnp.bfloat16)
    low = (values - high.astype(jnp.float32)).astype(jnp.bfloat16)
    return high, low


def host_halves(values):
    values = values.astype(np.float32)
    high = values.astype(jnp.bfloat16)
    low = (values - high.astype(np.float32)).astype(jnp.bfloat16)
    return high, low


def tables(length, block, blocks, padded_time):
    time = np.arange(length)

    def angle(frequency):
        return np.pi / length * ((frequency[:, None] * time[None, :]) % (2 * length))

    base = angle(np.arange(blocks) * block)
    coarse = np.zeros((blocks, 2, padded_time))
    coarse[:, 0, :length] = np.cos(base)
    coarse[:, 1, :length] = np.sin(base)
    coarse = coarse.reshape(blocks, 2 * padded_time)
    fine_angle = angle(np.arange(block))
    fine = np.zeros((2, SLOTS, 2, padded_time))
    fine[0, :block, 0, :length] = np.cos(fine_angle)
    fine[0, :block, 1, :length] = -np.sin(fine_angle)
    fine[1, :block, 0, :length] = -np.sin(fine_angle)
    fine[1, :block, 1, :length] = -np.cos(fine_angle)
    fine = fine.reshape(2, 2 * SLOTS, padded_time)
    full_angle = angle(np.arange(blocks * block)).reshape(blocks, block, length)
    full = np.zeros((padded_time, blocks, SLOTS, 2))
    full[:length, :, :block, 0] = np.cos(full_angle).transpose(2, 0, 1)
    full[:length, :, :block, 1] = -np.sin(full_angle).transpose(2, 0, 1)
    full = full.reshape(padded_time, blocks * 2 * SLOTS)
    coarse_high, coarse_low = host_halves(coarse)
    to_time = np.concatenate([coarse_high, coarse_high, coarse_low, coarse_low], axis=0)
    to_frequency = np.concatenate([coarse_high, coarse_low], axis=0).T.copy()
    full_high, full_low = host_halves(full)
    return full_high, full_low, to_time, to_frequency, fine.astype(np.float32)


def dot(a, b):
    return jnp.dot(a, b, preferred_element_type=jnp.float32)


def iota(shape, axis):
    return lax.broadcasted_iota(jnp.int32, shape, axis)


def source_kernel(vectors, raw, offsets, amplitude, full_high, full_low, out, padded, items):
    count, points, length = vectors.shape
    padded[...] = jnp.zeros_like(padded)
    for v in range(count):
        padded[v * points : (v + 1) * points, :length] = vectors[v]
    items[...] = jnp.zeros_like(items)
    near = raw.shape[0]
    weights = raw[...] / jnp.sum(raw[...], axis=0, keepdims=True)
    shifts = offsets[...].astype(jnp.float32)
    for k in range(near):
        lane = spare_lane(k)
        items[lane : lane + 1, :points] = weights[k : k + 1]
        lane = spare_lane(near + k)
        items[lane : lane + 1, :points] = shifts[k : k + 1]
    lane = spare_lane(2 * near)
    items[lane : lane + 1, :points] = amplitude[...]
    extra = items[...].T[:points]
    rows = count * points
    high, low = halves(padded[...])
    both = jnp.concatenate([high, low], axis=0)
    group_of_lane = iota((points, LANES), 1) // 32
    width = SPAN
    for start in range(0, full_high.shape[1], width):
        first = dot(both, full_high[:, start : start + width])
        second = dot(high, full_low[:, start : start + width])
        spectrum = first[:rows] + first[rows:] + second
        for tile in range(width // LANES):
            part = spectrum[:, tile * LANES : (tile + 1) * LANES]
            for e in range(4):
                block = extra
                for v in range(count):
                    piece = part[v * points : (v + 1) * points]
                    shift = (32 * (v - e)) % LANES
                    if shift:
                        piece = pltpu.roll(piece, shift, 1)
                    block = block + jnp.where(group_of_lane == v, piece, 0.0)
                out[start // 32 + tile * 4 + e] = block


def chebyshev(blocks, apply, put, load, store, coef, previous, current, total):
    def at(b):
        return slice(b * LANES, (b + 1) * LANES)

    for b in range(blocks):
        values = load(b)
        previous[at(b)] = values
        total[at(b)] = coef[0] * values
        put(0, b, values)
    degree = coef.shape[0] - 1
    for j in range(1, degree + 1):
        moved = apply((j - 1) % 2)
        for b in range(blocks):
            values = moved(b)
            if j > 1:
                values = 2.0 * values - previous[at(b)]
                if j < degree:
                    previous[at(b)] = current[at(b)]
            if j < degree:
                current[at(b)] = values
                total[at(b)] = total[at(b)] + coef[j] * values
                put(j % 2, b, values)
            else:
                store(b, total[at(b)] + coef[j] * values)


def item(table, index):
    lane = spare_lane(index)
    return table[:, lane : lane + 1]


def lane_frequency(shape):
    return (iota(shape, 1) % 32) // 2


def swapped(values):
    real = iota(values.shape, 1) % 2 == 0
    following = pltpu.roll(values, LANES - 1, 1)
    leading = pltpu.roll(values, 1, 1)
    return real, following, leading


def forward_kernel(
    near, received, coef, kernel, out, highs, lows, scatter, gather, previous, current, total, state, ready, held, sems
):
    pairs = sems.shape[0]
    copies = []
    for g in range(pairs):
        copies.append(
            pltpu.make_async_copy(kernel.at[:, pl.ds(2 * g, 2)], held.at[:, pl.ds(2 * g, 2)], sems.at[g])
        )
    early = (pairs + 1) // 2
    for copy in copies[:early]:
        copy.start()
    points = total.shape[0]
    blocks = points // LANES
    half = REACH // 2
    row = iota((SPAN - REACH, LANES), 0).astype(jnp.float32)
    column = iota((1, LANES), 1).astype(jnp.float32) + float(half)
    edge = jnp.zeros((half, LANES), jnp.float32)
    for b in range(blocks):
        turned = received[b * LANES : (b + 1) * LANES].T
        matrix = jnp.zeros((SPAN - REACH, LANES), jnp.float32)
        for k in range(near):
            lane, shift = spare_lane(k), spare_lane(near + k)
            target = turned[shift : shift + 1] + column
            matrix = matrix + jnp.where(row == target, turned[lane : lane + 1], 0.0)
        high, low = halves(jnp.concatenate([edge, matrix, edge], axis=0))
        both = jnp.concatenate([high, low], axis=1)
        scatter[b] = both
        gather[b] = both.T
    border = jnp.zeros((REACH, SPAN), jnp.bfloat16)
    for parity in range(2):
        state[parity, :REACH] = border
        state[parity, REACH + points :] = border

    def put(parity, b, values):
        high, low = halves(values)
        at = slice(REACH + b * LANES, REACH + (b + 1) * LANES)
        state[parity, at, :LANES] = high
        state[parity, at, LANES:] = low

    def apply(parity):
        def moved(b):
            product = dot(gather[b], state[parity, b * LANES : b * LANES + SPAN])
            return product[:LANES, :LANES] + product[:LANES, LANES:] + product[LANES:, :LANES]

        return moved

    def load(b):
        return received[b * LANES : (b + 1) * LANES]

    def store(b, values):
        at = slice(b * LANES, (b + 1) * LANES)
        high, low = halves(item(received[at], 2 * near) * values)
        ready[at, :LANES] = high
        ready[at, LANES:] = low

    chebyshev(blocks, apply, put, load, store, coef, previous, current, total)
    sensors = out.shape[0]
    of_lane = lane_frequency((sensors, LANES))
    direct = jnp.zeros((sensors, LANES), jnp.float32)
    crossed = jnp.zeros((sensors, LANES), jnp.float32)
    for copy in copies[:early]:
        copy.wait()
    for copy in copies[early:]:
        copy.start()
    for g in range(pairs):
        if g == early:
            for copy in copies[early:]:
                copy.wait()
        parts = []
        for f in (2 * g, 2 * g + 1):
            for c in range(2):
                high, low = halves(held[c, f])
                highs[c, f] = high
                lows[c, f] = low
                parts.extend((high, low))
        product = dot(jnp.concatenate(parts, axis=0), ready[...])
        for n, f in enumerate((2 * g, 2 * g + 1)):
            sums = []
            for c in range(2):
                at = (2 * n + c) * 2 * sensors
                top = product[at : at + sensors]
                bottom = product[at + sensors : at + 2 * sensors]
                sums.append(top[:, :LANES] + top[:, LANES:] + bottom[:, :LANES])
            direct = jnp.where(of_lane == f, sums[0], direct)
            crossed = jnp.where(of_lane == f, sums[1], crossed)
    real, following, leading = swapped(crossed)
    out[...] = direct + jnp.where(real, -following, leading)


def frequency_weight(block, blocks, length):
    shape = (blocks, LANES)
    slot = lane_frequency(shape)
    frequency = iota(shape, 0) * block + slot
    edge = (frequency == 0) | (frequency == length)
    weight = jnp.where(edge, 0.5 / length, 1.0 / length).astype(jnp.float32)
    return jnp.where((slot < block) & (frequency <= length), weight, 0.0)


def series(received, sets, blocks, weight, to_time, fine, each):
    padded_time = fine.shape[2]
    stacked = []
    for n in range(sets):
        values = received[pl.ds(n, blocks, stride=sets), :] * weight
        high = values.astype(jnp.bfloat16).astype(jnp.float32)
        low = values - high
        stacked.append(jnp.concatenate([high, low, high, low], axis=0).T.astype(jnp.bfloat16))
    product = dot(jnp.concatenate(stacked, axis=0), to_time[...])
    for n in range(sets):
        for v in range(4):
            at = n * LANES + v * 32
            rows = product[at : at + 32]
            terms = rows[:, :padded_time] * fine[0] + rows[:, padded_time:] * fine[1]
            each(n, v, jnp.sum(terms, axis=0, keepdims=True))


def sensor_kernel(block, length, received, noise, to_time, to_frequency, fine, out, moved):
    blocks = out.shape[0] // 2
    padded_time = fine.shape[2]
    weight = frequency_weight(block, blocks, length)

    def each(n, v, values):
        weighted = values * noise[n]
        for half in range(2):
            high, low = halves(weighted * fine[half])
            at = slice(half * padded_time, (half + 1) * padded_time)
            moved[n * SPAN + v * 32 : n * SPAN + v * 32 + 32, at] = high
            moved[n * SPAN + LANES + v * 32 : n * SPAN + LANES + v * 32 + 32, at] = low

    series(received, 2, blocks, weight, to_time, fine, each)
    product = dot(moved[...], to_frequency[...])
    for n in range(2):
        high = product[n * SPAN : n * SPAN + LANES]
        low = product[n * SPAN + LANES : (n + 1) * SPAN]
        result = high[:, :blocks] + high[:, blocks:] + low[:, :blocks]
        out[pl.ds(n, blocks, stride=2), :] = result.T


def adjoint_kernel(near, received, table, coef, highs, lows, scatter, out, previous, current, total, state, flat, grid):
    grid[...] = jnp.zeros_like(grid)
    chunks = highs.shape[3] // SPAN
    frequencies = highs.shape[1]
    points = total.shape[0]
    blocks = points // LANES
    values = received[...]
    real, following, leading = swapped(values)
    turned = jnp.concatenate([values, jnp.where(real, following, -leading)], axis=0).T
    high, low = halves(turned)
    pairs = frequencies // 2
    near_half = (iota((16, LANES), 0) % 4) // 2 == 0
    left = []
    for g in range(pairs):
        rows = []
        for part in (turned, turned - high.astype(jnp.float32)):
            picked = jnp.concatenate([part[32 * v + 4 * g : 32 * v + 4 * g + 4] for v in range(4)], axis=0)
            rows.append(
                jnp.concatenate([jnp.where(near_half, picked, 0.0), jnp.where(near_half, 0.0, picked)], axis=1)
            )
        left.append(jnp.concatenate(rows, axis=0).astype(jnp.bfloat16))
    for n in range(chunks):
        at = slice(n * SPAN, (n + 1) * SPAN)
        for g in range(pairs):
            order = [(c, f) for f in (2 * g, 2 * g + 1) for c in range(2)]
            first = dot(left[g], jnp.concatenate([highs[c, f, :, at] for c, f in order], axis=0))
            second = dot(left[g][:16], jnp.concatenate([lows[c, f, :, at] for c, f in order], axis=0))
            result = first[:16] + first[16:] + second
            for v in range(4):
                grid[32 * v + 4 * g : 32 * v + 4 * g + 4] = result[4 * v : 4 * v + 4]
        flat[n * SPAN : (n + 1) * SPAN] = grid[...].T

    blank = jnp.zeros((LANES, LANES), jnp.bfloat16)
    for parity in range(2):
        for b in range(blocks):
            state[parity, b, LANES:, LANES:] = blank

    def put(parity, b, values):
        high, low = halves(values)
        state[parity, b, :LANES, :LANES] = high
        state[parity, b, :LANES, LANES:] = low
        state[parity, b, LANES:, :LANES] = high

    half = REACH // 2

    def apply(parity):
        spreads = []
        for b in range(blocks):
            product = dot(scatter[b], state[parity, b])
            spreads.append(product[:, :LANES] + product[:, LANES:])

        def moved(b):
            middle = spreads[b][REACH : REACH + LANES]
            first, last = middle[:half], middle[LANES - half :]
            if b > 0:
                first = first + spreads[b - 1][REACH + LANES : REACH + LANES + half]
            if b < blocks - 1:
                last = last + spreads[b + 1][half:REACH]
            return jnp.concatenate([first, middle[half : LANES - half], last], axis=0)

        return moved

    def load(b):
        at = slice(b * LANES, (b + 1) * LANES)
        return item(table[at], 2 * near) * flat[at]

    def store(b, values):
        for i in range(4):
            for j in range(8):
                at = 16 * b + 4 * i
                out[j, at : at + 4] = values[32 * i + 4 * j : 32 * i + 4 * j + 4]

    chebyshev(blocks, apply, put, load, store, coef, previous, current, total)


def gradient_kernel(block, length, received, to_time, fine, out, once):
    blocks = received.shape[0] // 4
    weight = frequency_weight(block, blocks, length)

    def each(n, v, values):
        for tile in range(values.shape[1] // LANES):
            at = 16 * tile + 4 * v + n
            once[at : at + 1] = values[:, tile * LANES : (tile + 1) * LANES]

    series(received, 4, blocks, weight, to_time, fine, each)
    for copy in range(out.shape[0]):
        out[copy] = once[...]


def final_kernel(received, vectors, out):
    count, _, length = out.shape
    groups = received.shape[0]
    for tile in range(received.shape[1] // 16):
        lanes = min(LANES, length - tile * LANES)
        at = slice(tile * LANES, tile * LANES + lanes)
        for v in range(count):
            rows = [received[j, 16 * tile + 4 * v : 16 * tile + 4 * v + 4] for j in range(groups)]
            out[v, :, at] = vectors[v, :, at] + jnp.concatenate(rows, axis=0)[:, :lanes]


VMEM = pl.BlockSpec(memory_space=pltpu.VMEM)
SMEM = pl.BlockSpec(memory_space=pltpu.SMEM)
HBM = pl.BlockSpec(memory_space=pltpu.HBM)


def call(kernel, name, shapes, specs, scratch=(), fast=True):
    def result(shape, kind):
        return pltpu.VMEM(shape, kind) if fast else jax.ShapeDtypeStruct(shape, kind)

    outs = [result(shape, kind) for shape, kind in shapes]
    return pl.pallas_call(
        kernel,
        name=name,
        out_shape=outs if len(outs) > 1 else outs[0],
        in_specs=specs,
        out_specs=[VMEM] * len(outs) if len(outs) > 1 else VMEM,
        scratch_shapes=list(scratch),
        compiler_params=pltpu.CompilerParams(vmem_limit_bytes=28 * 1024 * 1024),
    )


def exchange(values, axis):
    return lax.all_to_all(values, axis, 0, 0, tiled=True)


def near_core(values):
    return pltpu.with_memory_space_constraint(values, pltpu.VMEM)


def in_place(values):
    return pltpu.with_memory_space_constraint(values, pltpu.HBM)


def body(vectors, kernel_hat, noise_prec, stencil_coefficients_raw, offsets, amplitude, cheb_coef):
    from functools import partial

    count, points, length = vectors.shape
    _, block, sensors, all_points = kernel_hat.shape
    near = offsets.shape[1]
    blocks = lax.axis_size("pts")
    groups = lax.axis_size("sens")
    padded_time = 512
    full_high, full_low, to_time, to_frequency, fine = tables(length, block, blocks, padded_time)
    f32, bf16 = jnp.float32, jnp.bfloat16
    to_time, to_frequency, fine = (near_core(jnp.asarray(table)) for table in (to_time, to_frequency, fine))
    bands = (all_points // LANES, SPAN, SPAN)
    grid_scratch = [
        pltpu.VMEM((all_points, LANES), f32),
        pltpu.VMEM((all_points, LANES), f32),
        pltpu.VMEM((all_points, LANES), f32),
    ]
    source = call(
        source_kernel,
        "source",
        [((blocks, points, LANES), f32)],
        [VMEM] * 6,
        [pltpu.VMEM((count * points, padded_time), f32), pltpu.VMEM((LANES, LANES), f32)],
    )(
        *map(
            in_place,
            (
                vectors,
                stencil_coefficients_raw.T,
                offsets.T,
                amplitude.reshape(1, points),
                jnp.asarray(full_high),
                jnp.asarray(full_low),
            ),
        )
    )
    spectrum = near_core(exchange(source, "pts").reshape(all_points, LANES))
    data, kernel_high, kernel_low, scatter = call(
        partial(forward_kernel, near),
        "forward",
        [((sensors, LANES), f32), (kernel_hat.shape, bf16), (kernel_hat.shape, bf16), (bands, bf16)],
        [VMEM, SMEM, HBM],
        [pltpu.VMEM(bands, bf16)]
        + grid_scratch
        + [
            pltpu.VMEM((2, all_points + 2 * REACH, SPAN), bf16),
            pltpu.VMEM((all_points, SPAN), bf16),
            pltpu.VMEM(kernel_hat.shape, f32),
            pltpu.SemaphoreType.DMA((block // 2,)),
        ],
    )(spectrum, cheb_coef, in_place(kernel_hat))
    data = near_core(exchange(data.reshape(blocks, sensors // blocks, LANES), "pts").reshape(sensors, LANES))
    back = call(
        partial(sensor_kernel, block, length),
        "sensor",
        [((sensors, LANES), f32)],
        [VMEM, SMEM, VMEM, VMEM, VMEM],
        [pltpu.VMEM((2 * SPAN, 2 * padded_time), bf16)],
    )(data, noise_prec, to_time, to_frequency, fine)
    back = near_core(exchange(back.reshape(blocks, sensors // blocks, LANES), "pts").reshape(sensors, LANES))
    partial_sums = call(
        partial(adjoint_kernel, near),
        "adjoint",
        [((groups, all_points // groups, LANES), f32)],
        [VMEM, VMEM, SMEM, VMEM, VMEM, VMEM],
        grid_scratch + [pltpu.VMEM((2,) + bands, bf16), pltpu.VMEM((all_points, LANES), f32), pltpu.VMEM((LANES, SPAN), f32)],
    )(back, spectrum, cheb_coef, near_core(kernel_high), near_core(kernel_low), near_core(scatter))
    summed = jnp.sum(exchange(partial_sums, "sens"), axis=0)
    share = points // groups
    moved = near_core(exchange(summed.reshape(blocks, share, LANES), "pts").reshape(blocks * share, LANES))
    gradient = call(
        partial(gradient_kernel, block, length),
        "gradient",
        [((groups, share * count * padded_time // LANES, LANES), f32)],
        [VMEM, VMEM, VMEM],
        [pltpu.VMEM((share * count * padded_time // LANES, LANES), f32)],
    )(moved, to_time, fine)
    gathered = near_core(exchange(gradient, "sens"))
    return call(final_kernel, "final", [((count, points, length), f32)], [VMEM, VMEM], fast=False)(gathered, vectors)


def solution(mesh):
    placed = (
        P(None, "pts", None),
        P(None, "pts", "sens", None),
        P(("sens", "pts")),
        P("pts", None),
        P("pts", None),
        P("pts"),
        P(),
    )
    return jax.shard_map(
        body, mesh=mesh, in_specs=placed, out_specs=P(None, "pts", None), check_vma=False
    )
```

```python
import numpy as np
import jax
import jax.numpy as jnp
from jax import lax
from jax.experimental import pallas as pl
from jax.experimental.pallas import tpu as pltpu
from jax.sharding import PartitionSpec as P

LANES = 128
SPAN = 256
REACH = 64
SLOTS = 16


def spare_lane(item):
    return 32 * (item // 4) + 28 + item % 4


def halves(values):
    high = values.astype(jnp.bfloat16)
    low = (values - high.astype(jnp.float32)).astype(jnp.bfloat16)
    return high, low


def host_halves(values):
    values = values.astype(np.float32)
    high = values.astype(jnp.bfloat16)
    low = (values - high.astype(np.float32)).astype(jnp.bfloat16)
    return high, low


def tables(length, block, blocks, padded_time):
    time = np.arange(length)

    def angle(frequency):
        return np.pi / length * ((frequency[:, None] * time[None, :]) % (2 * length))

    base = angle(np.arange(blocks) * block)
    coarse = np.zeros((blocks, 2, padded_time))
    coarse[:, 0, :length] = np.cos(base)
    coarse[:, 1, :length] = np.sin(base)
    coarse = coarse.reshape(blocks, 2 * padded_time)
    fine_angle = angle(np.arange(block))
    fine = np.zeros((2, SLOTS, 2, padded_time))
    fine[0, :block, 0, :length] = np.cos(fine_angle)
    fine[0, :block, 1, :length] = -np.sin(fine_angle)
    fine[1, :block, 0, :length] = -np.sin(fine_angle)
    fine[1, :block, 1, :length] = -np.cos(fine_angle)
    fine = fine.reshape(2, 2 * SLOTS, padded_time)
    full_angle = angle(np.arange(blocks * block)).reshape(blocks, block, length)
    full = np.zeros((padded_time, blocks, SLOTS, 2))
    full[:length, :, :block, 0] = np.cos(full_angle).transpose(2, 0, 1)
    full[:length, :, :block, 1] = -np.sin(full_angle).transpose(2, 0, 1)
    full = full.reshape(padded_time, blocks * 2 * SLOTS)
    coarse_high, coarse_low = host_halves(coarse)
    to_time = np.concatenate([coarse_high, coarse_high, coarse_low, coarse_low], axis=0)
    to_frequency = np.concatenate([coarse_high, coarse_low], axis=0).T.copy()
    full_high, full_low = host_halves(full)
    return full_high, full_low, to_time, to_frequency, fine.astype(np.float32)


def dot(a, b):
    return jnp.dot(a, b, preferred_element_type=jnp.float32)


def iota(shape, axis):
    return lax.broadcasted_iota(jnp.int32, shape, axis)


def source_kernel(vectors, raw, offsets, amplitude, full_high, full_low, out, padded, items):
    count, points, length = vectors.shape
    padded[...] = jnp.zeros_like(padded)
    for v in range(count):
        padded[v * points : (v + 1) * points, :length] = vectors[v]
    items[...] = jnp.zeros_like(items)
    near = raw.shape[0]
    weights = raw[...] / jnp.sum(raw[...], axis=0, keepdims=True)
    shifts = offsets[...].astype(jnp.float32)
    for k in range(near):
        lane = spare_lane(k)
        items[lane : lane + 1, :points] = weights[k : k + 1]
        lane = spare_lane(near + k)
        items[lane : lane + 1, :points] = shifts[k : k + 1]
    lane = spare_lane(2 * near)
    items[lane : lane + 1, :points] = amplitude[...]
    extra = items[...].T[:points]
    rows = count * points
    high, low = halves(padded[...])
    both = jnp.concatenate([high, low], axis=0)
    group_of_lane = iota((points, LANES), 1) // 32
    width = SPAN
    for start in range(0, full_high.shape[1], width):
        first = dot(both, full_high[:, start : start + width])
        second = dot(high, full_low[:, start : start + width])
        spectrum = first[:rows] + first[rows:] + second
        for tile in range(width // LANES):
            part = spectrum[:, tile * LANES : (tile + 1) * LANES]
            for e in range(4):
                block = extra
                for v in range(count):
                    piece = part[v * points : (v + 1) * points]
                    shift = (32 * (v - e)) % LANES
                    if shift:
                        piece = pltpu.roll(piece, shift, 1)
                    block = block + jnp.where(group_of_lane == v, piece, 0.0)
                out[start // 32 + tile * 4 + e] = block


def chebyshev(blocks, apply, put, load, store, coef, previous, current, total):
    def at(b):
        return slice(b * LANES, (b + 1) * LANES)

    for b in range(blocks):
        values = load(b)
        previous[at(b)] = values
        total[at(b)] = coef[0] * values
        put(0, b, values)
    degree = coef.shape[0] - 1
    for j in range(1, degree + 1):
        moved = apply((j - 1) % 2)
        for b in range(blocks):
            values = moved(b)
            if j > 1:
                values = 2.0 * values - previous[at(b)]
                if j < degree:
                    previous[at(b)] = current[at(b)]
            if j < degree:
                current[at(b)] = values
                total[at(b)] = total[at(b)] + coef[j] * values
                put(j % 2, b, values)
            else:
                store(b, total[at(b)] + coef[j] * values)


def item(table, index):
    lane = spare_lane(index)
    return table[:, lane : lane + 1]


def lane_frequency(shape):
    return (iota(shape, 1) % 32) // 2


def swapped(values):
    real = iota(values.shape, 1) % 2 == 0
    following = pltpu.roll(values, LANES - 1, 1)
    leading = pltpu.roll(values, 1, 1)
    return real, following, leading


def forward_kernel(
    near, received, coef, kernel, out, highs, lows, scatter, gather, previous, current, total, state, ready, held, sems
):
    pairs = sems.shape[0]
    copies = []
    for g in range(pairs):
        copies.append(
            pltpu.make_async_copy(kernel.at[:, pl.ds(2 * g, 2)], held.at[:, pl.ds(2 * g, 2)], sems.at[g])
        )
    early = pairs - 2
    for copy in copies[:early]:
        copy.start()
    points = total.shape[0]
    blocks = points // LANES
    half = REACH // 2
    row = iota((SPAN - REACH, LANES), 0).astype(jnp.float32)
    column = iota((1, LANES), 1).astype(jnp.float32) + float(half)
    edge = jnp.zeros((half, LANES), jnp.float32)
    for b in range(blocks):
        turned = received[b * LANES : (b + 1) * LANES].T
        matrix = jnp.zeros((SPAN - REACH, LANES), jnp.float32)
        for k in range(near):
            lane, shift = spare_lane(k), spare_lane(near + k)
            target = turned[shift : shift + 1] + column
            matrix = matrix + jnp.where(row == target, turned[lane : lane + 1], 0.0)
        high, low = halves(jnp.concatenate([edge, matrix, edge], axis=0))
        both = jnp.concatenate([high, low], axis=1)
        scatter[b] = both
        gather[b] = both.T
    border = jnp.zeros((REACH, SPAN), jnp.bfloat16)
    for parity in range(2):
        state[parity, :REACH] = border
        state[parity, REACH + points :] = border

    def put(parity, b, values):
        high, low = halves(values)
        at = slice(REACH + b * LANES, REACH + (b + 1) * LANES)
        state[parity, at, :LANES] = high
        state[parity, at, LANES:] = low

    def apply(parity):
        def moved(b):
            product = dot(gather[b], state[parity, b * LANES : b * LANES + SPAN])
            return product[:LANES, :LANES] + product[:LANES, LANES:] + product[LANES:, :LANES]

        return moved

    def load(b):
        return received[b * LANES : (b + 1) * LANES]

    def store(b, values):
        at = slice(b * LANES, (b + 1) * LANES)
        high, low = halves(item(received[at], 2 * near) * values)
        ready[at, :LANES] = high
        ready[at, LANES:] = low

    chebyshev(blocks, apply, put, load, store, coef, previous, current, total)
    sensors = out.shape[0]
    of_lane = lane_frequency((sensors, LANES))
    direct = jnp.zeros((sensors, LANES), jnp.float32)
    crossed = jnp.zeros((sensors, LANES), jnp.float32)
    for copy in copies[:early]:
        copy.wait()
    for copy in copies[early:]:
        copy.start()
    for g in range(pairs):
        if g == early:
            for copy in copies[early:]:
                copy.wait()
        parts = []
        for f in (2 * g, 2 * g + 1):
            for c in range(2):
                high, low = halves(held[c, f])
                highs[c, f] = high
                lows[c, f] = low
                parts.extend((high, low))
        product = dot(jnp.concatenate(parts, axis=0), ready[...])
        for n, f in enumerate((2 * g, 2 * g + 1)):
            sums = []
            for c in range(2):
                at = (2 * n + c) * 2 * sensors
                top = product[at : at + sensors]
                bottom = product[at + sensors : at + 2 * sensors]
                sums.append(top[:, :LANES] + top[:, LANES:] + bottom[:, :LANES])
            direct = jnp.where(of_lane == f, sums[0], direct)
            crossed = jnp.where(of_lane == f, sums[1], crossed)
    real, following, leading = swapped(crossed)
    out[...] = direct + jnp.where(real, -following, leading)


def frequency_weight(block, blocks, length):
    shape = (blocks, LANES)
    slot = lane_frequency(shape)
    frequency = iota(shape, 0) * block + slot
    edge = (frequency == 0) | (frequency == length)
    weight = jnp.where(edge, 0.5 / length, 1.0 / length).astype(jnp.float32)
    return jnp.where((slot < block) & (frequency <= length), weight, 0.0)


def series(received, sets, blocks, weight, to_time, fine, each):
    padded_time = fine.shape[2]
    stacked = []
    for n in range(sets):
        values = received[pl.ds(n, blocks, stride=sets), :] * weight
        high = values.astype(jnp.bfloat16).astype(jnp.float32)
        low = values - high
        stacked.append(jnp.concatenate([high, low, high, low], axis=0).T.astype(jnp.bfloat16))
    product = dot(jnp.concatenate(stacked, axis=0), to_time[...])
    for n in range(sets):
        for v in range(4):
            at = n * LANES + v * 32
            rows = product[at : at + 32]
            terms = rows[:, :padded_time] * fine[0] + rows[:, padded_time:] * fine[1]
            each(n, v, jnp.sum(terms, axis=0, keepdims=True))


def sensor_kernel(block, length, received, noise, to_time, to_frequency, fine, out, moved):
    blocks = out.shape[0] // 2
    padded_time = fine.shape[2]
    weight = frequency_weight(block, blocks, length)

    def each(n, v, values):
        weighted = values * noise[n]
        for half in range(2):
            high, low = halves(weighted * fine[half])
            at = slice(half * padded_time, (half + 1) * padded_time)
            moved[n * SPAN + v * 32 : n * SPAN + v * 32 + 32, at] = high
            moved[n * SPAN + LANES + v * 32 : n * SPAN + LANES + v * 32 + 32, at] = low

    series(received, 2, blocks, weight, to_time, fine, each)
    product = dot(moved[...], to_frequency[...])
    for n in range(2):
        high = product[n * SPAN : n * SPAN + LANES]
        low = product[n * SPAN + LANES : (n + 1) * SPAN]
        result = high[:, :blocks] + high[:, blocks:] + low[:, :blocks]
        out[pl.ds(n, blocks, stride=2), :] = result.T


def adjoint_kernel(near, received, table, coef, highs, lows, scatter, out, previous, current, total, state, flat, grid):
    grid[...] = jnp.zeros_like(grid)
    chunks = highs.shape[3] // SPAN
    frequencies = highs.shape[1]
    points = total.shape[0]
    blocks = points // LANES
    values = received[...]
    real, following, leading = swapped(values)
    turned = jnp.concatenate([values, jnp.where(real, following, -leading)], axis=0).T
    high, low = halves(turned)
    pairs = frequencies // 2
    near_half = (iota((16, LANES), 0) % 4) // 2 == 0
    left = []
    for g in range(pairs):
        rows = []
        for part in (turned, turned - high.astype(jnp.float32)):
            picked = jnp.concatenate([part[32 * v + 4 * g : 32 * v + 4 * g + 4] for v in range(4)], axis=0)
            rows.append(
                jnp.concatenate([jnp.where(near_half, picked, 0.0), jnp.where(near_half, 0.0, picked)], axis=1)
            )
        left.append(jnp.concatenate(rows, axis=0).astype(jnp.bfloat16))
    for n in range(chunks):
        at = slice(n * SPAN, (n + 1) * SPAN)
        for g in range(pairs):
            order = [(c, f) for f in (2 * g, 2 * g + 1) for c in range(2)]
            first = dot(left[g], jnp.concatenate([highs[c, f, :, at] for c, f in order], axis=0))
            second = dot(left[g][:16], jnp.concatenate([lows[c, f, :, at] for c, f in order], axis=0))
            result = first[:16] + first[16:] + second
            for v in range(4):
                grid[32 * v + 4 * g : 32 * v + 4 * g + 4] = result[4 * v : 4 * v + 4]
        flat[n * SPAN : (n + 1) * SPAN] = grid[...].T

    blank = jnp.zeros((LANES, LANES), jnp.bfloat16)
    for parity in range(2):
        for b in range(blocks):
            state[parity, b, LANES:, LANES:] = blank

    def put(parity, b, values):
        high, low = halves(values)
        state[parity, b, :LANES, :LANES] = high
        state[parity, b, :LANES, LANES:] = low
        state[parity, b, LANES:, :LANES] = high

    half = REACH // 2

    def apply(parity):
        spreads = []
        for b in range(blocks):
            product = dot(scatter[b], state[parity, b])
            spreads.append(product[:, :LANES] + product[:, LANES:])

        def moved(b):
            middle = spreads[b][REACH : REACH + LANES]
            first, last = middle[:half], middle[LANES - half :]
            if b > 0:
                first = first + spreads[b - 1][REACH + LANES : REACH + LANES + half]
            if b < blocks - 1:
                last = last + spreads[b + 1][half:REACH]
            return jnp.concatenate([first, middle[half : LANES - half], last], axis=0)

        return moved

    def load(b):
        at = slice(b * LANES, (b + 1) * LANES)
        return item(table[at], 2 * near) * flat[at]

    def store(b, values):
        for i in range(4):
            for j in range(8):
                at = 16 * b + 4 * i
                out[j, at : at + 4] = values[32 * i + 4 * j : 32 * i + 4 * j + 4]

    chebyshev(blocks, apply, put, load, store, coef, previous, current, total)


def gradient_kernel(block, length, received, to_time, fine, out, once):
    blocks = received.shape[0] // 4
    weight = frequency_weight(block, blocks, length)

    def each(n, v, values):
        for tile in range(values.shape[1] // LANES - 1):
            at = 16 * tile + 4 * v + n
            once[at : at + 1] = values[:, tile * LANES : (tile + 1) * LANES]
        tail = values[:, values.shape[1] - LANES :]
        at = 48 + 4 * (v // 2) + n
        if v % 2:
            once[at : at + 1] = once[at : at + 1] + pltpu.roll(tail, LANES // 2, 1)
        else:
            once[at : at + 1] = tail

    series(received, 4, blocks, weight, to_time, fine, each)
    for copy in range(out.shape[0]):
        out[copy] = once[...]


def final_kernel(received, vectors, out):
    count, _, length = out.shape
    groups = received.shape[0]
    for tile in range(3):
        at = slice(tile * LANES, (tile + 1) * LANES)
        for v in range(count):
            rows = [received[j, 16 * tile + 4 * v : 16 * tile + 4 * v + 4] for j in range(groups)]
            out[v, :, at] = vectors[v, :, at] + jnp.concatenate(rows, axis=0)
    for v in range(count):
        first = 48 + 4 * (v // 2)
        rows = jnp.concatenate([received[j, first : first + 4] for j in range(groups)], axis=0)
        if v % 2:
            rows = pltpu.roll(rows, LANES // 2, 1)
        out[v, :, 3 * LANES :] = vectors[v, :, 3 * LANES :] + rows[:, : length - 3 * LANES]


VMEM = pl.BlockSpec(memory_space=pltpu.VMEM)
SMEM = pl.BlockSpec(memory_space=pltpu.SMEM)
HBM = pl.BlockSpec(memory_space=pltpu.HBM)


def call(kernel, name, shapes, specs, scratch=(), fast=True):
    def result(shape, kind):
        return pltpu.VMEM(shape, kind) if fast else jax.ShapeDtypeStruct(shape, kind)

    outs = [result(shape, kind) for shape, kind in shapes]
    return pl.pallas_call(
        kernel,
        name=name,
        out_shape=outs if len(outs) > 1 else outs[0],
        in_specs=specs,
        out_specs=[VMEM] * len(outs) if len(outs) > 1 else VMEM,
        scratch_shapes=list(scratch),
        compiler_params=pltpu.CompilerParams(vmem_limit_bytes=28 * 1024 * 1024),
    )


def exchange(values, axis):
    return lax.all_to_all(values, axis, 0, 0, tiled=True)


def near_core(values):
    return pltpu.with_memory_space_constraint(values, pltpu.VMEM)


def in_place(values):
    return pltpu.with_memory_space_constraint(values, pltpu.HBM)


def body(vectors, kernel_hat, noise_prec, stencil_coefficients_raw, offsets, amplitude, cheb_coef):
    from functools import partial

    count, points, length = vectors.shape
    _, block, sensors, all_points = kernel_hat.shape
    near = offsets.shape[1]
    blocks = lax.axis_size("pts")
    groups = lax.axis_size("sens")
    padded_time = 512
    full_high, full_low, to_time, to_frequency, fine = tables(length, block, blocks, padded_time)
    f32, bf16 = jnp.float32, jnp.bfloat16
    to_time, to_frequency, fine = (near_core(jnp.asarray(table)) for table in (to_time, to_frequency, fine))
    bands = (all_points // LANES, SPAN, SPAN)
    grid_scratch = [
        pltpu.VMEM((all_points, LANES), f32),
        pltpu.VMEM((all_points, LANES), f32),
        pltpu.VMEM((all_points, LANES), f32),
    ]
    source = call(
        source_kernel,
        "source",
        [((blocks, points, LANES), f32)],
        [VMEM] * 6,
        [pltpu.VMEM((count * points, padded_time), f32), pltpu.VMEM((LANES, LANES), f32)],
    )(
        *map(
            in_place,
            (
                vectors,
                stencil_coefficients_raw.T,
                offsets.T,
                amplitude.reshape(1, points),
                jnp.asarray(full_high),
                jnp.asarray(full_low),
            ),
        )
    )
    spectrum = near_core(exchange(source, "pts").reshape(all_points, LANES))
    data, kernel_high, kernel_low, scatter = call(
        partial(forward_kernel, near),
        "forward",
        [((sensors, LANES), f32), (kernel_hat.shape, bf16), (kernel_hat.shape, bf16), (bands, bf16)],
        [VMEM, SMEM, HBM],
        [pltpu.VMEM(bands, bf16)]
        + grid_scratch
        + [
            pltpu.VMEM((2, all_points + 2 * REACH, SPAN), bf16),
            pltpu.VMEM((all_points, SPAN), bf16),
            pltpu.VMEM(kernel_hat.shape, f32),
            pltpu.SemaphoreType.DMA((block // 2,)),
        ],
    )(spectrum, cheb_coef, in_place(kernel_hat))
    data = near_core(exchange(data.reshape(blocks, sensors // blocks, LANES), "pts").reshape(sensors, LANES))
    back = call(
        partial(sensor_kernel, block, length),
        "sensor",
        [((sensors, LANES), f32)],
        [VMEM, SMEM, VMEM, VMEM, VMEM],
        [pltpu.VMEM((2 * SPAN, 2 * padded_time), bf16)],
    )(data, noise_prec, to_time, to_frequency, fine)
    back = near_core(exchange(back.reshape(blocks, sensors // blocks, LANES), "pts").reshape(sensors, LANES))
    partial_sums = call(
        partial(adjoint_kernel, near),
        "adjoint",
        [((groups, all_points // groups, LANES), f32)],
        [VMEM, VMEM, SMEM, VMEM, VMEM, VMEM],
        grid_scratch + [pltpu.VMEM((2,) + bands, bf16), pltpu.VMEM((all_points, LANES), f32), pltpu.VMEM((LANES, SPAN), f32)],
    )(back, spectrum, cheb_coef, near_core(kernel_high), near_core(kernel_low), near_core(scatter))
    summed = jnp.sum(exchange(partial_sums, "sens"), axis=0)
    share = points // groups
    moved = near_core(exchange(summed.reshape(blocks, share, LANES), "pts").reshape(blocks * share, LANES))
    gradient = call(
        partial(gradient_kernel, block, length),
        "gradient",
        [((groups, 56, LANES), f32)],
        [VMEM, VMEM, VMEM],
        [pltpu.VMEM((56, LANES), f32)],
    )(moved, to_time, fine)
    gathered = near_core(exchange(gradient, "sens"))
    return call(final_kernel, "final", [((count, points, length), f32)], [VMEM, VMEM], fast=False)(gathered, vectors)


def solution(mesh):
    placed = (
        P(None, "pts", None),
        P(None, "pts", "sens", None),
        P(("sens", "pts")),
        P("pts", None),
        P("pts", None),
        P("pts"),
        P(),
    )
    return jax.shard_map(
        body, mesh=mesh, in_specs=placed, out_specs=P(None, "pts", None), check_vma=False
    )
```

```python
import numpy as np
import jax
import jax.numpy as jnp
from jax import lax
from jax.experimental import pallas as pl
from jax.experimental.pallas import tpu as pltpu
from jax.sharding import PartitionSpec as P

LANES = 128
SPAN = 256
REACH = 64
SLOTS = 16


def spare_lane(item):
    return 32 * (item // 4) + 28 + item % 4


def halves(values):
    high = values.astype(jnp.bfloat16)
    low = (values - high.astype(jnp.float32)).astype(jnp.bfloat16)
    return high, low


def host_halves(values):
    values = values.astype(np.float32)
    high = values.astype(jnp.bfloat16)
    low = (values - high.astype(np.float32)).astype(jnp.bfloat16)
    return high, low


def tables(length, block, blocks, padded_time):
    time = np.arange(length)

    def angle(frequency):
        return np.pi / length * ((frequency[:, None] * time[None, :]) % (2 * length))

    base = angle(np.arange(blocks) * block)
    coarse = np.zeros((blocks, 2, padded_time))
    coarse[:, 0, :length] = np.cos(base)
    coarse[:, 1, :length] = np.sin(base)
    coarse = coarse.reshape(blocks, 2 * padded_time)
    fine_angle = angle(np.arange(block))
    fine = np.zeros((2, SLOTS, 2, padded_time))
    fine[0, :block, 0, :length] = np.cos(fine_angle)
    fine[0, :block, 1, :length] = -np.sin(fine_angle)
    fine[1, :block, 0, :length] = -np.sin(fine_angle)
    fine[1, :block, 1, :length] = -np.cos(fine_angle)
    fine = fine.reshape(2, 2 * SLOTS, padded_time)
    full_angle = angle(np.arange(blocks * block)).reshape(blocks, block, length)
    rows = -(-length // 16) * 16
    full = np.zeros((rows, blocks, SLOTS, 2))
    full[:length, :, :block, 0] = np.cos(full_angle).transpose(2, 0, 1)
    full[:length, :, :block, 1] = -np.sin(full_angle).transpose(2, 0, 1)
    full = full.reshape(rows, blocks * 2 * SLOTS)
    coarse_high, coarse_low = host_halves(coarse)
    to_time = np.concatenate([coarse_high, coarse_high, coarse_low, coarse_low], axis=0)
    to_frequency = np.concatenate([coarse_high, coarse_low], axis=0).T.copy()
    full_high, full_low = host_halves(full)
    return full_high, full_low, to_time, to_frequency, fine.astype(np.float32)


def dot(a, b):
    return jnp.dot(a, b, preferred_element_type=jnp.float32)


def iota(shape, axis):
    return lax.broadcasted_iota(jnp.int32, shape, axis)


def source_kernel(vectors, raw, offsets, amplitude, coef, full_high, full_low, out, padded, items):
    count, points, length = vectors.shape
    padded[...] = jnp.zeros_like(padded)
    for v in range(count):
        padded[v * points : (v + 1) * points, :length] = vectors[v]
    items[...] = jnp.zeros_like(items)
    near = raw.shape[0]
    weights = raw[...] / jnp.sum(raw[...], axis=0, keepdims=True)
    shifts = offsets[...].astype(jnp.float32)
    for k in range(near):
        lane = spare_lane(k)
        items[lane : lane + 1, :points] = weights[k : k + 1]
        lane = spare_lane(near + k)
        items[lane : lane + 1, :points] = shifts[k : k + 1]
    lane = spare_lane(2 * near)
    items[lane : lane + 1, :points] = amplitude[...]
    lane = spare_lane(2 * near + 1)
    items[lane : lane + 1, : coef.shape[1]] = coef[...]
    extra = items[...].T[:points]
    rows = count * points
    high, low = halves(padded[:, : full_high.shape[0]])
    both = jnp.concatenate([high, low], axis=0)
    group_of_lane = iota((points, LANES), 1) // 32
    width = SPAN
    for start in range(0, full_high.shape[1], width):
        first = dot(both, full_high[:, start : start + width])
        second = dot(high, full_low[:, start : start + width])
        spectrum = first[:rows] + first[rows:] + second
        for tile in range(width // LANES):
            part = spectrum[:, tile * LANES : (tile + 1) * LANES]
            for e in range(4):
                block = extra
                for v in range(count):
                    piece = part[v * points : (v + 1) * points]
                    shift = (32 * (v - e)) % LANES
                    if shift:
                        piece = pltpu.roll(piece, shift, 1)
                    block = block + jnp.where(group_of_lane == v, piece, 0.0)
                out[start // 32 + tile * 4 + e] = block


def chebyshev(blocks, apply, put, load, store, coef, previous, current, total):
    degree = len(coef) - 1

    def at(b):
        return slice(b * LANES, (b + 1) * LANES)

    for b in range(blocks):
        values = load(b)
        previous[at(b)] = values
        total[at(b)] = coef[0] * values
        put(0, b, values)
    for j in range(1, degree + 1):
        moved = apply((j - 1) % 2)
        for b in range(blocks):
            values = moved(b)
            if j > 1:
                values = 2.0 * values - previous[at(b)]
                if j < degree:
                    previous[at(b)] = current[at(b)]
            if j < degree:
                current[at(b)] = values
                total[at(b)] = total[at(b)] + coef[j] * values
                put(j % 2, b, values)
            else:
                store(b, total[at(b)] + coef[j] * values)


def item(table, index):
    lane = spare_lane(index)
    return table[:, lane : lane + 1]


def coefficients(table, near, degree):
    lane = spare_lane(2 * near + 1)
    return [table[j : j + 1, lane : lane + 1] for j in range(degree + 1)]


def lane_frequency(shape):
    return (iota(shape, 1) % 32) // 2


def swapped(values):
    real = iota(values.shape, 1) % 2 == 0
    following = pltpu.roll(values, LANES - 1, 1)
    leading = pltpu.roll(values, 1, 1)
    return real, following, leading


def forward_kernel(
    near, degree, received, kernel, out, highs, lows, scatter, gather, previous, current, total, state, ready, held, sems
):
    pairs = sems.shape[0]
    copies = []
    for g in range(pairs):
        copies.append(
            pltpu.make_async_copy(kernel.at[:, pl.ds(2 * g, 2)], held.at[:, pl.ds(2 * g, 2)], sems.at[g])
        )
    early = pairs - 2
    for copy in copies[:early]:
        copy.start()
    points = total.shape[0]
    blocks = points // LANES
    half = REACH // 2
    row = iota((SPAN - REACH, LANES), 0).astype(jnp.float32)
    column = iota((1, LANES), 1).astype(jnp.float32) + float(half)
    edge = jnp.zeros((half, LANES), jnp.float32)
    for b in range(blocks):
        turned = received[b * LANES : (b + 1) * LANES].T
        matrix = jnp.zeros((SPAN - REACH, LANES), jnp.float32)
        for k in range(near):
            lane, shift = spare_lane(k), spare_lane(near + k)
            target = turned[shift : shift + 1] + column
            matrix = matrix + jnp.where(row == target, turned[lane : lane + 1], 0.0)
        high, low = halves(jnp.concatenate([edge, matrix, edge], axis=0))
        both = jnp.concatenate([high, low], axis=1)
        scatter[b] = both
        gather[b] = both.T
    border = jnp.zeros((REACH, SPAN), jnp.bfloat16)
    for parity in range(2):
        state[parity, :REACH] = border
        state[parity, REACH + points :] = border

    def put(parity, b, values):
        high, low = halves(values)
        at = slice(REACH + b * LANES, REACH + (b + 1) * LANES)
        state[parity, at, :LANES] = high
        state[parity, at, LANES:] = low

    def apply(parity):
        def moved(b):
            product = dot(gather[b], state[parity, b * LANES : b * LANES + SPAN])
            return product[:LANES, :LANES] + product[:LANES, LANES:] + product[LANES:, :LANES]

        return moved

    def load(b):
        return received[b * LANES : (b + 1) * LANES]

    def store(b, values):
        at = slice(b * LANES, (b + 1) * LANES)
        high, low = halves(item(received[at], 2 * near) * values)
        ready[at, :LANES] = high
        ready[at, LANES:] = low

    coef = coefficients(received, near, degree)
    chebyshev(blocks, apply, put, load, store, coef, previous, current, total)
    sensors = out.shape[0]
    of_lane = lane_frequency((sensors, LANES))
    direct = jnp.zeros((sensors, LANES), jnp.float32)
    crossed = jnp.zeros((sensors, LANES), jnp.float32)
    for copy in copies[:early]:
        copy.wait()
    for copy in copies[early:]:
        copy.start()
    for g in range(pairs):
        if g == early:
            for copy in copies[early:]:
                copy.wait()
        parts = []
        for f in (2 * g, 2 * g + 1):
            for c in range(2):
                high, low = halves(held[c, f])
                highs[c, f] = high
                lows[c, f] = low
                parts.extend((high, low))
        product = dot(jnp.concatenate(parts, axis=0), ready[...])
        for n, f in enumerate((2 * g, 2 * g + 1)):
            sums = []
            for c in range(2):
                at = (2 * n + c) * 2 * sensors
                top = product[at : at + sensors]
                bottom = product[at + sensors : at + 2 * sensors]
                sums.append(top[:, :LANES] + top[:, LANES:] + bottom[:, :LANES])
            direct = jnp.where(of_lane == f, sums[0], direct)
            crossed = jnp.where(of_lane == f, sums[1], crossed)
    real, following, leading = swapped(crossed)
    out[...] = direct + jnp.where(real, -following, leading)


def frequency_weight(block, blocks, length):
    shape = (blocks, LANES)
    slot = lane_frequency(shape)
    frequency = iota(shape, 0) * block + slot
    edge = (frequency == 0) | (frequency == length)
    weight = jnp.where(edge, 0.5 / length, 1.0 / length).astype(jnp.float32)
    return jnp.where((slot < block) & (frequency <= length), weight, 0.0)


def series(received, sets, blocks, weight, to_time, fine, each):
    padded_time = fine.shape[2]
    stacked = []
    for n in range(sets):
        values = received[pl.ds(n, blocks, stride=sets), :] * weight
        high = values.astype(jnp.bfloat16).astype(jnp.float32)
        low = values - high
        stacked.append(jnp.concatenate([high, low, high, low], axis=0).T.astype(jnp.bfloat16))
    product = dot(jnp.concatenate(stacked, axis=0), to_time[...])
    for n in range(sets):
        for v in range(4):
            at = n * LANES + v * 32
            rows = product[at : at + 32]
            terms = rows[:, :padded_time] * fine[0] + rows[:, padded_time:] * fine[1]
            each(n, v, jnp.sum(terms, axis=0, keepdims=True))


def sensor_kernel(block, length, received, noise, to_time, to_frequency, fine, out, moved):
    blocks = out.shape[0] // 2
    padded_time = fine.shape[2]
    weight = frequency_weight(block, blocks, length)

    def each(n, v, values):
        weighted = values * noise[n]
        for half in range(2):
            high, low = halves(weighted * fine[half])
            at = slice(half * padded_time, (half + 1) * padded_time)
            moved[n * SPAN + v * 32 : n * SPAN + v * 32 + 32, at] = high
            moved[n * SPAN + LANES + v * 32 : n * SPAN + LANES + v * 32 + 32, at] = low

    series(received, 2, blocks, weight, to_time, fine, each)
    product = dot(moved[...], to_frequency[...])
    for n in range(2):
        high = product[n * SPAN : n * SPAN + LANES]
        low = product[n * SPAN + LANES : (n + 1) * SPAN]
        result = high[:, :blocks] + high[:, blocks:] + low[:, :blocks]
        out[pl.ds(n, blocks, stride=2), :] = result.T


def adjoint_kernel(near, degree, received, table, highs, lows, scatter, out, previous, current, total, state, flat, grid):
    grid[...] = jnp.zeros_like(grid)
    chunks = highs.shape[3] // SPAN
    frequencies = highs.shape[1]
    points = total.shape[0]
    blocks = points // LANES
    values = received[...]
    real, following, leading = swapped(values)
    turned = jnp.concatenate([values, jnp.where(real, following, -leading)], axis=0).T
    high, low = halves(turned)
    pairs = frequencies // 2
    near_half = (iota((16, LANES), 0) % 4) // 2 == 0
    left = []
    for g in range(pairs):
        rows = []
        for part in (turned, turned - high.astype(jnp.float32)):
            picked = jnp.concatenate([part[32 * v + 4 * g : 32 * v + 4 * g + 4] for v in range(4)], axis=0)
            rows.append(
                jnp.concatenate([jnp.where(near_half, picked, 0.0), jnp.where(near_half, 0.0, picked)], axis=1)
            )
        left.append(jnp.concatenate(rows, axis=0).astype(jnp.bfloat16))
    for n in range(chunks):
        at = slice(n * SPAN, (n + 1) * SPAN)
        for g in range(pairs):
            order = [(c, f) for f in (2 * g, 2 * g + 1) for c in range(2)]
            first = dot(left[g], jnp.concatenate([highs[c, f, :, at] for c, f in order], axis=0))
            second = dot(left[g][:16], jnp.concatenate([lows[c, f, :, at] for c, f in order], axis=0))
            result = first[:16] + first[16:] + second
            for v in range(4):
                grid[32 * v + 4 * g : 32 * v + 4 * g + 4] = result[4 * v : 4 * v + 4]
        flat[n * SPAN : (n + 1) * SPAN] = grid[...].T

    blank = jnp.zeros((LANES, LANES), jnp.bfloat16)
    for parity in range(2):
        for b in range(blocks):
            state[parity, b, LANES:, LANES:] = blank

    def put(parity, b, values):
        high, low = halves(values)
        state[parity, b, :LANES, :LANES] = high
        state[parity, b, :LANES, LANES:] = low
        state[parity, b, LANES:, :LANES] = high

    half = REACH // 2

    def apply(parity):
        spreads = []
        for b in range(blocks):
            product = dot(scatter[b], state[parity, b])
            spreads.append(product[:, :LANES] + product[:, LANES:])

        def moved(b):
            middle = spreads[b][REACH : REACH + LANES]
            first, last = middle[:half], middle[LANES - half :]
            if b > 0:
                first = first + spreads[b - 1][REACH + LANES : REACH + LANES + half]
            if b < blocks - 1:
                last = last + spreads[b + 1][half:REACH]
            return jnp.concatenate([first, middle[half : LANES - half], last], axis=0)

        return moved

    def load(b):
        at = slice(b * LANES, (b + 1) * LANES)
        return item(table[at], 2 * near) * flat[at]

    def store(b, values):
        for i in range(4):
            for j in range(8):
                at = 16 * b + 4 * i
                out[j, at : at + 4] = values[32 * i + 4 * j : 32 * i + 4 * j + 4]

    coef = coefficients(table, near, degree)
    chebyshev(blocks, apply, put, load, store, coef, previous, current, total)


def gradient_kernel(block, length, received, to_time, fine, out, once):
    blocks = received.shape[0] // 4
    weight = frequency_weight(block, blocks, length)

    def each(n, v, values):
        for tile in range(values.shape[1] // LANES - 1):
            at = 16 * tile + 4 * v + n
            once[at : at + 1] = values[:, tile * LANES : (tile + 1) * LANES]
        tail = values[:, values.shape[1] - LANES :]
        at = 48 + 4 * (v // 2) + n
        if v % 2:
            once[at : at + 1] = once[at : at + 1] + pltpu.roll(tail, LANES // 2, 1)
        else:
            once[at : at + 1] = tail

    series(received, 4, blocks, weight, to_time, fine, each)
    for copy in range(out.shape[0]):
        out[copy] = once[...]


def final_kernel(received, vectors, out):
    count, _, length = out.shape
    groups = received.shape[0]
    for tile in range(3):
        at = slice(tile * LANES, (tile + 1) * LANES)
        for v in range(count):
            rows = [received[j, 16 * tile + 4 * v : 16 * tile + 4 * v + 4] for j in range(groups)]
            out[v, :, at] = vectors[v, :, at] + jnp.concatenate(rows, axis=0)
    for v in range(count):
        first = 48 + 4 * (v // 2)
        rows = jnp.concatenate([received[j, first : first + 4] for j in range(groups)], axis=0)
        if v % 2:
            rows = pltpu.roll(rows, LANES // 2, 1)
        out[v, :, 3 * LANES :] = vectors[v, :, 3 * LANES :] + rows[:, : length - 3 * LANES]


VMEM = pl.BlockSpec(memory_space=pltpu.VMEM)
SMEM = pl.BlockSpec(memory_space=pltpu.SMEM)
HBM = pl.BlockSpec(memory_space=pltpu.HBM)


def call(kernel, name, shapes, specs, scratch=(), fast=True):
    def result(shape, kind):
        return pltpu.VMEM(shape, kind) if fast else jax.ShapeDtypeStruct(shape, kind)

    outs = [result(shape, kind) for shape, kind in shapes]
    return pl.pallas_call(
        kernel,
        name=name,
        out_shape=outs if len(outs) > 1 else outs[0],
        in_specs=specs,
        out_specs=[VMEM] * len(outs) if len(outs) > 1 else VMEM,
        scratch_shapes=list(scratch),
        compiler_params=pltpu.CompilerParams(vmem_limit_bytes=28 * 1024 * 1024),
    )


def exchange(values, axis):
    return lax.all_to_all(values, axis, 0, 0, tiled=True)


def near_core(values):
    return pltpu.with_memory_space_constraint(values, pltpu.VMEM)


def in_place(values):
    return pltpu.with_memory_space_constraint(values, pltpu.HBM)


def body(vectors, kernel_hat, noise_prec, stencil_coefficients_raw, offsets, amplitude, cheb_coef):
    from functools import partial

    count, points, length = vectors.shape
    _, block, sensors, all_points = kernel_hat.shape
    near = offsets.shape[1]
    degree = cheb_coef.shape[0] - 1
    blocks = lax.axis_size("pts")
    groups = lax.axis_size("sens")
    padded_time = 512
    full_high, full_low, to_time, to_frequency, fine = tables(length, block, blocks, padded_time)
    f32, bf16 = jnp.float32, jnp.bfloat16
    to_time, to_frequency, fine = (near_core(jnp.asarray(table)) for table in (to_time, to_frequency, fine))
    bands = (all_points // LANES, SPAN, SPAN)
    grid_scratch = [
        pltpu.VMEM((all_points, LANES), f32),
        pltpu.VMEM((all_points, LANES), f32),
        pltpu.VMEM((all_points, LANES), f32),
    ]
    source = call(
        source_kernel,
        "source",
        [((blocks, points, LANES), f32)],
        [VMEM] * 7,
        [pltpu.VMEM((count * points, padded_time), f32), pltpu.VMEM((LANES, LANES), f32)],
    )(
        *map(
            in_place,
            (
                vectors,
                stencil_coefficients_raw.T,
                offsets.T,
                amplitude.reshape(1, points),
                cheb_coef.reshape(1, -1),
                jnp.asarray(full_high),
                jnp.asarray(full_low),
            ),
        )
    )
    spectrum = near_core(exchange(source, "pts").reshape(all_points, LANES))
    data, kernel_high, kernel_low, scatter = call(
        partial(forward_kernel, near, degree),
        "forward",
        [((sensors, LANES), f32), (kernel_hat.shape, bf16), (kernel_hat.shape, bf16), (bands, bf16)],
        [VMEM, HBM],
        [pltpu.VMEM(bands, bf16)]
        + grid_scratch
        + [
            pltpu.VMEM((2, all_points + 2 * REACH, SPAN), bf16),
            pltpu.VMEM((all_points, SPAN), bf16),
            pltpu.VMEM(kernel_hat.shape, f32),
            pltpu.SemaphoreType.DMA((block // 2,)),
        ],
    )(spectrum, in_place(kernel_hat))
    data = near_core(exchange(data.reshape(blocks, sensors // blocks, LANES), "pts").reshape(sensors, LANES))
    back = call(
        partial(sensor_kernel, block, length),
        "sensor",
        [((sensors, LANES), f32)],
        [VMEM, SMEM, VMEM, VMEM, VMEM],
        [pltpu.VMEM((2 * SPAN, 2 * padded_time), bf16)],
    )(data, noise_prec, to_time, to_frequency, fine)
    back = near_core(exchange(back.reshape(blocks, sensors // blocks, LANES), "pts").reshape(sensors, LANES))
    partial_sums = call(
        partial(adjoint_kernel, near, degree),
        "adjoint",
        [((groups, all_points // groups, LANES), f32)],
        [VMEM, VMEM, VMEM, VMEM, VMEM],
        grid_scratch + [pltpu.VMEM((2,) + bands, bf16), pltpu.VMEM((all_points, LANES), f32), pltpu.VMEM((LANES, SPAN), f32)],
    )(back, spectrum, near_core(kernel_high), near_core(kernel_low), near_core(scatter))
    summed = jnp.sum(exchange(partial_sums, "sens"), axis=0)
    share = points // groups
    moved = near_core(exchange(summed.reshape(blocks, share, LANES), "pts").reshape(blocks * share, LANES))
    gradient = call(
        partial(gradient_kernel, block, length),
        "gradient",
        [((groups, 56, LANES), f32)],
        [VMEM, VMEM, VMEM],
        [pltpu.VMEM((56, LANES), f32)],
    )(moved, to_time, fine)
    gathered = near_core(exchange(gradient, "sens"))
    return call(final_kernel, "final", [((count, points, length), f32)], [VMEM, VMEM], fast=False)(gathered, vectors)


def solution(mesh):
    placed = (
        P(None, "pts", None),
        P(None, "pts", "sens", None),
        P(("sens", "pts")),
        P("pts", None),
        P("pts", None),
        P("pts"),
        P(),
    )
    return jax.shard_map(
        body, mesh=mesh, in_specs=placed, out_specs=P(None, "pts", None), check_vma=False
    )
```

```python
import numpy as np
import jax
import jax.numpy as jnp
from jax import lax
from jax.experimental import pallas as pl
from jax.experimental.pallas import tpu as pltpu
from jax.sharding import PartitionSpec as P

LANES = 128
SPAN = 256
REACH = 64
SLOTS = 16


def spare_lane(item):
    return 32 * (item // 4) + 28 + item % 4


def halves(values):
    high = values.astype(jnp.bfloat16)
    low = (values - high.astype(jnp.float32)).astype(jnp.bfloat16)
    return high, low


def host_halves(values):
    values = values.astype(np.float32)
    high = values.astype(jnp.bfloat16)
    low = (values - high.astype(np.float32)).astype(jnp.bfloat16)
    return high, low


def tables(length, block, blocks, padded_time):
    time = np.arange(length)

    def angle(frequency):
        return np.pi / length * ((frequency[:, None] * time[None, :]) % (2 * length))

    base = angle(np.arange(blocks) * block)
    coarse = np.zeros((blocks, 2, padded_time))
    coarse[:, 0, :length] = np.cos(base)
    coarse[:, 1, :length] = np.sin(base)
    coarse = coarse.reshape(blocks, 2 * padded_time)
    fine_angle = angle(np.arange(block))
    fine = np.zeros((2, SLOTS, 2, padded_time))
    fine[0, :block, 0, :length] = np.cos(fine_angle)
    fine[0, :block, 1, :length] = -np.sin(fine_angle)
    fine[1, :block, 0, :length] = -np.sin(fine_angle)
    fine[1, :block, 1, :length] = -np.cos(fine_angle)
    fine = fine.reshape(2, 2 * SLOTS, padded_time)
    full_angle = angle(np.arange(blocks * block)).reshape(blocks, block, length)
    rows = -(-length // 16) * 16
    full = np.zeros((rows, blocks, SLOTS, 2))
    full[:length, :, :block, 0] = np.cos(full_angle).transpose(2, 0, 1)
    full[:length, :, :block, 1] = -np.sin(full_angle).transpose(2, 0, 1)
    full = full.reshape(rows, blocks * 2 * SLOTS)
    coarse_high, coarse_low = host_halves(coarse)
    to_time = np.concatenate([coarse_high, coarse_high, coarse_low, coarse_low], axis=0)
    to_frequency = np.concatenate([coarse_high, coarse_low], axis=0).T.copy()
    full_high, full_low = host_halves(full)
    return full_high, full_low, to_time, to_frequency, fine.astype(np.float32)


def dot(a, b):
    return jnp.dot(a, b, preferred_element_type=jnp.float32)


def iota(shape, axis):
    return lax.broadcasted_iota(jnp.int32, shape, axis)


def source_kernel(vectors, raw, offsets, amplitude, coef, full_high, full_low, out, padded, items):
    count, points, length = vectors.shape
    padded[...] = jnp.zeros_like(padded)
    for v in range(count):
        padded[v * points : (v + 1) * points, :length] = vectors[v]
    items[...] = jnp.zeros_like(items)
    near = raw.shape[0]
    weights = raw[...] / jnp.sum(raw[...], axis=0, keepdims=True)
    shifts = offsets[...].astype(jnp.float32)
    for k in range(near):
        lane = spare_lane(k)
        items[lane : lane + 1, :points] = weights[k : k + 1]
        lane = spare_lane(near + k)
        items[lane : lane + 1, :points] = shifts[k : k + 1]
    lane = spare_lane(2 * near)
    items[lane : lane + 1, :points] = amplitude[...]
    lane = spare_lane(2 * near + 1)
    items[lane : lane + 1, : coef.shape[1]] = coef[...]
    extra = items[...].T[:points]
    rows = count * points
    high, low = halves(padded[:, : full_high.shape[0]])
    both = jnp.concatenate([high, low], axis=0)
    group_of_lane = iota((points, LANES), 1) // 32
    width = SPAN
    for start in range(0, full_high.shape[1], width):
        first = dot(both, full_high[:, start : start + width])
        second = dot(high, full_low[:, start : start + width])
        spectrum = first[:rows] + first[rows:] + second
        for tile in range(width // LANES):
            part = spectrum[:, tile * LANES : (tile + 1) * LANES]
            for e in range(4):
                block = extra
                for v in range(count):
                    piece = part[v * points : (v + 1) * points]
                    shift = (32 * (v - e)) % LANES
                    if shift:
                        piece = pltpu.roll(piece, shift, 1)
                    block = block + jnp.where(group_of_lane == v, piece, 0.0)
                out[start // 32 + tile * 4 + e] = block


def chebyshev(blocks, apply, put, load, store, coef, previous, current, total):
    degree = len(coef) - 1

    def at(b):
        return slice(b * LANES, (b + 1) * LANES)

    for b in range(blocks):
        values = load(b)
        previous[at(b)] = values
        total[at(b)] = coef[0] * values
        put(0, b, values)
    for j in range(1, degree + 1):
        moved = apply((j - 1) % 2)
        for b in range(blocks):
            values = moved(b)
            if j > 1:
                values = 2.0 * values - previous[at(b)]
                if j < degree:
                    previous[at(b)] = current[at(b)]
            if j < degree:
                current[at(b)] = values
                total[at(b)] = total[at(b)] + coef[j] * values
                put(j % 2, b, values)
            else:
                store(b, total[at(b)] + coef[j] * values)


def item(table, index):
    lane = spare_lane(index)
    return table[:, lane : lane + 1]


def coefficients(table, near, degree):
    lane = spare_lane(2 * near + 1)
    return [table[j : j + 1, lane : lane + 1] for j in range(degree + 1)]


def lane_frequency(shape):
    return (iota(shape, 1) % 32) // 2


def swapped(values):
    real = iota(values.shape, 1) % 2 == 0
    following = pltpu.roll(values, LANES - 1, 1)
    leading = pltpu.roll(values, 1, 1)
    return real, following, leading


def forward_kernel(
    near, degree, received, kernel, out, highs, lows, scatter, gather, previous, current, total, state, ready, held, sems
):
    pairs = sems.shape[0]
    copies = []
    for g in range(pairs):
        copies.append(
            pltpu.make_async_copy(kernel.at[:, pl.ds(2 * g, 2)], held.at[:, pl.ds(2 * g, 2)], sems.at[g])
        )
    early = pairs - 2
    for copy in copies[:early]:
        copy.start()
    points = total.shape[0]
    blocks = points // LANES
    half = REACH // 2
    row = iota((SPAN - REACH, LANES), 0).astype(jnp.float32)
    column = iota((1, LANES), 1).astype(jnp.float32) + float(half)
    edge = jnp.zeros((half, LANES), jnp.float32)
    for b in range(blocks):
        turned = received[b * LANES : (b + 1) * LANES].T
        matrix = jnp.zeros((SPAN - REACH, LANES), jnp.float32)
        for k in range(near):
            lane, shift = spare_lane(k), spare_lane(near + k)
            target = turned[shift : shift + 1] + column
            matrix = matrix + jnp.where(row == target, turned[lane : lane + 1], 0.0)
        high, low = halves(jnp.concatenate([edge, matrix, edge], axis=0))
        both = jnp.concatenate([high, low], axis=1)
        scatter[b] = both
        gather[b] = both.T
    border = jnp.zeros((REACH, SPAN), jnp.bfloat16)
    for parity in range(2):
        state[parity, :REACH] = border
        state[parity, REACH + points :] = border

    def put(parity, b, values):
        high, low = halves(values)
        at = slice(REACH + b * LANES, REACH + (b + 1) * LANES)
        state[parity, at, :LANES] = high
        state[parity, at, LANES:] = low

    def apply(parity):
        def moved(b):
            product = dot(gather[b], state[parity, b * LANES : b * LANES + SPAN])
            return product[:LANES, :LANES] + product[:LANES, LANES:] + product[LANES:, :LANES]

        return moved

    def load(b):
        return received[b * LANES : (b + 1) * LANES]

    def store(b, values):
        at = slice(b * LANES, (b + 1) * LANES)
        high, low = halves(item(received[at], 2 * near) * values)
        ready[at, :LANES] = high
        ready[at, LANES:] = low

    coef = coefficients(received, near, degree)
    chebyshev(blocks, apply, put, load, store, coef, previous, current, total)
    sensors = out.shape[0]
    of_lane = lane_frequency((sensors, LANES))
    direct = jnp.zeros((sensors, LANES), jnp.float32)
    crossed = jnp.zeros((sensors, LANES), jnp.float32)
    for copy in copies[:early]:
        copy.wait()
    for copy in copies[early:]:
        copy.start()
    for g in range(pairs):
        if g == early:
            for copy in copies[early:]:
                copy.wait()
        parts = []
        for f in (2 * g, 2 * g + 1):
            for c in range(2):
                high, low = halves(held[c, f])
                highs[c, f] = high
                lows[c, f] = low
                parts.extend((high, low))
        product = dot(jnp.concatenate(parts, axis=0), ready[...])
        for n, f in enumerate((2 * g, 2 * g + 1)):
            sums = []
            for c in range(2):
                at = (2 * n + c) * 2 * sensors
                top = product[at : at + sensors]
                bottom = product[at + sensors : at + 2 * sensors]
                sums.append(top[:, :LANES] + top[:, LANES:] + bottom[:, :LANES])
            direct = jnp.where(of_lane == f, sums[0], direct)
            crossed = jnp.where(of_lane == f, sums[1], crossed)
    real, following, leading = swapped(crossed)
    out[...] = direct + jnp.where(real, -following, leading)


def frequency_weight(block, blocks, length):
    shape = (blocks, LANES)
    slot = lane_frequency(shape)
    frequency = iota(shape, 0) * block + slot
    edge = (frequency == 0) | (frequency == length)
    weight = jnp.where(edge, 0.5 / length, 1.0 / length).astype(jnp.float32)
    return jnp.where((slot < block) & (frequency <= length), weight, 0.0)


def series(received, sets, blocks, weight, to_time, fine, each):
    padded_time = fine.shape[2]
    stacked = []
    for n in range(sets):
        values = received[pl.ds(n, blocks, stride=sets), :] * weight
        high = values.astype(jnp.bfloat16).astype(jnp.float32)
        low = values - high
        stacked.append(jnp.concatenate([high, low, high, low], axis=0).T.astype(jnp.bfloat16))
    product = dot(jnp.concatenate(stacked, axis=0), to_time[...])
    for n in range(sets):
        for v in range(4):
            at = n * LANES + v * 32
            rows = product[at : at + 32]
            terms = rows[:, :padded_time] * fine[0] + rows[:, padded_time:] * fine[1]
            each(n, v, jnp.sum(terms, axis=0, keepdims=True))


def sensor_kernel(block, length, received, noise, to_time, to_frequency, fine, out, moved):
    blocks = out.shape[0] // 2
    padded_time = fine.shape[2]
    weight = frequency_weight(block, blocks, length)

    def each(n, v, values):
        weighted = values * noise[:, n : n + 1]
        for half in range(2):
            high, low = halves(weighted * fine[half])
            at = slice(half * padded_time, (half + 1) * padded_time)
            moved[n * SPAN + v * 32 : n * SPAN + v * 32 + 32, at] = high
            moved[n * SPAN + LANES + v * 32 : n * SPAN + LANES + v * 32 + 32, at] = low

    series(received, 2, blocks, weight, to_time, fine, each)
    product = dot(moved[...], to_frequency[...])
    for n in range(2):
        high = product[n * SPAN : n * SPAN + LANES]
        low = product[n * SPAN + LANES : (n + 1) * SPAN]
        result = high[:, :blocks] + high[:, blocks:] + low[:, :blocks]
        out[pl.ds(n, blocks, stride=2), :] = result.T


def adjoint_kernel(near, degree, received, table, highs, lows, scatter, out, previous, current, total, state, flat, grid):
    grid[...] = jnp.zeros_like(grid)
    chunks = highs.shape[3] // SPAN
    frequencies = highs.shape[1]
    points = total.shape[0]
    blocks = points // LANES
    values = received[...]
    real, following, leading = swapped(values)
    turned = jnp.concatenate([values, jnp.where(real, following, -leading)], axis=0).T
    high, low = halves(turned)
    pairs = frequencies // 2
    near_half = (iota((16, LANES), 0) % 4) // 2 == 0
    left = []
    for g in range(pairs):
        rows = []
        for part in (turned, turned - high.astype(jnp.float32)):
            picked = jnp.concatenate([part[32 * v + 4 * g : 32 * v + 4 * g + 4] for v in range(4)], axis=0)
            rows.append(
                jnp.concatenate([jnp.where(near_half, picked, 0.0), jnp.where(near_half, 0.0, picked)], axis=1)
            )
        left.append(jnp.concatenate(rows, axis=0).astype(jnp.bfloat16))
    for n in range(chunks):
        at = slice(n * SPAN, (n + 1) * SPAN)
        for g in range(pairs):
            order = [(c, f) for f in (2 * g, 2 * g + 1) for c in range(2)]
            first = dot(left[g], jnp.concatenate([highs[c, f, :, at] for c, f in order], axis=0))
            second = dot(left[g][:16], jnp.concatenate([lows[c, f, :, at] for c, f in order], axis=0))
            result = first[:16] + first[16:] + second
            for v in range(4):
                grid[32 * v + 4 * g : 32 * v + 4 * g + 4] = result[4 * v : 4 * v + 4]
        flat[n * SPAN : (n + 1) * SPAN] = grid[...].T

    blank = jnp.zeros((LANES, LANES), jnp.bfloat16)
    for parity in range(2):
        for b in range(blocks):
            state[parity, b, LANES:, LANES:] = blank

    def put(parity, b, values):
        high, low = halves(values)
        state[parity, b, :LANES, :LANES] = high
        state[parity, b, :LANES, LANES:] = low
        state[parity, b, LANES:, :LANES] = high

    half = REACH // 2

    def apply(parity):
        spreads = []
        for b in range(blocks):
            product = dot(scatter[b], state[parity, b])
            spreads.append(product[:, :LANES] + product[:, LANES:])

        def moved(b):
            middle = spreads[b][REACH : REACH + LANES]
            first, last = middle[:half], middle[LANES - half :]
            if b > 0:
                first = first + spreads[b - 1][REACH + LANES : REACH + LANES + half]
            if b < blocks - 1:
                last = last + spreads[b + 1][half:REACH]
            return jnp.concatenate([first, middle[half : LANES - half], last], axis=0)

        return moved

    def load(b):
        at = slice(b * LANES, (b + 1) * LANES)
        return item(table[at], 2 * near) * flat[at]

    def store(b, values):
        for i in range(4):
            for j in range(8):
                at = 16 * b + 4 * i
                out[j, at : at + 4] = values[32 * i + 4 * j : 32 * i + 4 * j + 4]

    coef = coefficients(table, near, degree)
    chebyshev(blocks, apply, put, load, store, coef, previous, current, total)


def gradient_kernel(block, length, received, to_time, fine, out, once):
    blocks = received.shape[0] // 4
    weight = frequency_weight(block, blocks, length)

    def each(n, v, values):
        for tile in range(values.shape[1] // LANES - 1):
            at = 16 * tile + 4 * v + n
            once[at : at + 1] = values[:, tile * LANES : (tile + 1) * LANES]
        tail = values[:, values.shape[1] - LANES :]
        at = 48 + 4 * (v // 2) + n
        if v % 2:
            once[at : at + 1] = once[at : at + 1] + pltpu.roll(tail, LANES // 2, 1)
        else:
            once[at : at + 1] = tail

    series(received, 4, blocks, weight, to_time, fine, each)
    for copy in range(out.shape[0]):
        out[copy] = once[...]


def final_kernel(received, vectors, out):
    count, _, length = out.shape
    groups = received.shape[0]
    for tile in range(3):
        at = slice(tile * LANES, (tile + 1) * LANES)
        for v in range(count):
            rows = [received[j, 16 * tile + 4 * v : 16 * tile + 4 * v + 4] for j in range(groups)]
            out[v, :, at] = vectors[v, :, at] + jnp.concatenate(rows, axis=0)
    for v in range(count):
        first = 48 + 4 * (v // 2)
        rows = jnp.concatenate([received[j, first : first + 4] for j in range(groups)], axis=0)
        if v % 2:
            rows = pltpu.roll(rows, LANES // 2, 1)
        out[v, :, 3 * LANES :] = vectors[v, :, 3 * LANES :] + rows[:, : length - 3 * LANES]


VMEM = pl.BlockSpec(memory_space=pltpu.VMEM)
HBM = pl.BlockSpec(memory_space=pltpu.HBM)


def call(kernel, name, shapes, specs, scratch=(), fast=True):
    def result(shape, kind):
        return pltpu.VMEM(shape, kind) if fast else jax.ShapeDtypeStruct(shape, kind)

    outs = [result(shape, kind) for shape, kind in shapes]
    return pl.pallas_call(
        kernel,
        name=name,
        out_shape=outs if len(outs) > 1 else outs[0],
        in_specs=specs,
        out_specs=[VMEM] * len(outs) if len(outs) > 1 else VMEM,
        scratch_shapes=list(scratch),
        compiler_params=pltpu.CompilerParams(vmem_limit_bytes=28 * 1024 * 1024),
    )


def exchange(values, axis):
    return lax.all_to_all(values, axis, 0, 0, tiled=True)


def near_core(values):
    return pltpu.with_memory_space_constraint(values, pltpu.VMEM)


def in_place(values):
    return pltpu.with_memory_space_constraint(values, pltpu.HBM)


def body(vectors, kernel_hat, noise_prec, stencil_coefficients_raw, offsets, amplitude, cheb_coef):
    from functools import partial

    count, points, length = vectors.shape
    _, block, sensors, all_points = kernel_hat.shape
    near = offsets.shape[1]
    degree = cheb_coef.shape[0] - 1
    blocks = lax.axis_size("pts")
    groups = lax.axis_size("sens")
    padded_time = 512
    full_high, full_low, to_time, to_frequency, fine = tables(length, block, blocks, padded_time)
    f32, bf16 = jnp.float32, jnp.bfloat16
    to_time, to_frequency, fine = (near_core(jnp.asarray(table)) for table in (to_time, to_frequency, fine))
    bands = (all_points // LANES, SPAN, SPAN)
    grid_scratch = [
        pltpu.VMEM((all_points, LANES), f32),
        pltpu.VMEM((all_points, LANES), f32),
        pltpu.VMEM((all_points, LANES), f32),
    ]
    source = call(
        source_kernel,
        "source",
        [((blocks, points, LANES), f32)],
        [VMEM] * 7,
        [pltpu.VMEM((count * points, padded_time), f32), pltpu.VMEM((LANES, LANES), f32)],
    )(
        *map(
            in_place,
            (
                vectors,
                stencil_coefficients_raw.T,
                offsets.T,
                amplitude.reshape(1, points),
                cheb_coef.reshape(1, -1),
                jnp.asarray(full_high),
                jnp.asarray(full_low),
            ),
        )
    )
    spectrum = near_core(exchange(source, "pts").reshape(all_points, LANES))
    data, kernel_high, kernel_low, scatter = call(
        partial(forward_kernel, near, degree),
        "forward",
        [((sensors, LANES), f32), (kernel_hat.shape, bf16), (kernel_hat.shape, bf16), (bands, bf16)],
        [VMEM, HBM],
        [pltpu.VMEM(bands, bf16)]
        + grid_scratch
        + [
            pltpu.VMEM((2, all_points + 2 * REACH, SPAN), bf16),
            pltpu.VMEM((all_points, SPAN), bf16),
            pltpu.VMEM(kernel_hat.shape, f32),
            pltpu.SemaphoreType.DMA((block // 2,)),
        ],
    )(spectrum, in_place(kernel_hat))
    data = near_core(exchange(data.reshape(blocks, sensors // blocks, LANES), "pts").reshape(sensors, LANES))
    back = call(
        partial(sensor_kernel, block, length),
        "sensor",
        [((sensors, LANES), f32)],
        [VMEM, VMEM, VMEM, VMEM, VMEM],
        [pltpu.VMEM((2 * SPAN, 2 * padded_time), bf16)],
    )(data, near_core(noise_prec.reshape(1, -1)), to_time, to_frequency, fine)
    back = near_core(exchange(back.reshape(blocks, sensors // blocks, LANES), "pts").reshape(sensors, LANES))
    partial_sums = call(
        partial(adjoint_kernel, near, degree),
        "adjoint",
        [((groups, all_points // groups, LANES), f32)],
        [VMEM, VMEM, VMEM, VMEM, VMEM],
        grid_scratch + [pltpu.VMEM((2,) + bands, bf16), pltpu.VMEM((all_points, LANES), f32), pltpu.VMEM((LANES, SPAN), f32)],
    )(back, spectrum, near_core(kernel_high), near_core(kernel_low), near_core(scatter))
    summed = jnp.sum(exchange(partial_sums, "sens"), axis=0)
    share = points // groups
    moved = near_core(exchange(summed.reshape(blocks, share, LANES), "pts").reshape(blocks * share, LANES))
    gradient = call(
        partial(gradient_kernel, block, length),
        "gradient",
        [((groups, 56, LANES), f32)],
        [VMEM, VMEM, VMEM],
        [pltpu.VMEM((56, LANES), f32)],
    )(moved, to_time, fine)
    gathered = near_core(exchange(gradient, "sens"))
    return call(final_kernel, "final", [((count, points, length), f32)], [VMEM, VMEM], fast=False)(gathered, vectors)


def solution(mesh):
    placed = (
        P(None, "pts", None),
        P(None, "pts", "sens", None),
        P(("sens", "pts")),
        P("pts", None),
        P("pts", None),
        P("pts"),
        P(),
    )
    return jax.shard_map(
        body, mesh=mesh, in_specs=placed, out_specs=P(None, "pts", None), check_vma=False
    )
```
